32 devices in a mesh: segment: 2 (over y), expert: 16 (over z, x, core).
Axes of the slice: x: 2, y: 2, z: 4, core: 2. Of those that a mesh axis runs over, the one named last changes fastest.
Arguments:
- hidden: bfloat16 [2, 512, 2048], P('segment', 'expert'), may hold values from -6 to 6
- memory: bfloat16 [2, 512, 2048], P('segment', 'expert'), may hold values from -6 to 6
- lengths: int32 [2, 16], P('segment', 'expert'), may hold values from 1 to 32, as said below
- memory_lengths: int32 [2, 16], P('segment', 'expert'), may hold values from 1 to 32, as said below
- routes: int32 [2, 512, 2], P('segment', 'expert'), may hold values from 0 to 3, all different within a row; in each aligned block of 32 rows (0 to 31, 32 to 63, ..., all dimensions but the last counted through in order) at most 20 rows name the same one
- norm_gain: float32 [2, 3, 2048], P('segment'), may hold values from 0.5 to 1.5, as said below
- router: bfloat16 [2, 2048, 4], P('segment'), may hold values from -0.26516504 to 0.26516504, as said below
- w_in: bfloat16 [2, 2048, 16384], P('segment', None, 'expert'), may hold values from -0.13258252 to 0.13258252, as said below
- w_out: bfloat16 [2, 16384, 2048], P('segment', 'expert'), may hold values from -0.125 to 0.125, as said below
- shortlist: bfloat16 [2, 2048, 512], P('segment'), may hold values from -0.375 to 0.375
- student: float32 [2, 512, 512], P('segment', 'expert'), may hold values from -15 to 15
- targets: int32 [2, 512], P('segment', 'expert'), may hold values from 0 to 511
Outputs:
- layer_out: bfloat16 [2, 512, 2048], P('segment', 'expert')
- loss: float32 [], replicated
The draws below stay inside these ranges and needn't reach their ends.
Inputs may be any that keep to these rules, and one draw needn't show every extreme that they name: `lengths`: every sequence has at least one position; the first sequence of each section has 32. `memory_lengths`: every sequence has at least one position; the first sequence of each section has 32. `routes`: A token's two experts differ. In the 32 rows of one device no expert is named more than 20 times, a bound that some block reaches. `norm_gain`: equal in all encoder sections, and equal in all decoder sections. `router`: equal in all encoder sections, and equal in all decoder sections. `w_in`: equal in all encoder sections, and equal in all decoder sections. `w_out`: equal in all encoder sections, and equal in all decoder sections.
All inputs are finite; a program needn't handle non-finite values.
Results may differ from the reference program's by a relative error of at most 0.0049.
Values may be sent and summed in bfloat16 or wider, within the bound.
A program may use at most 64 MiB of HBM per device.

```python
import math
import jax
import jax.numpy as jnp
import numpy as np
from jax import lax

D = 2048
HEADS = 16
HEAD_DIM = 128
FF = 4096
EXPERTS = 4
VOCW = 512
LEN = 32
TOK_DEV = 32
CAP = 20
SEQS = 16
TOKENS = 512
N_SEGMENT = 2
N_EXPERT = 16


def lengths_common(key):
    drawn = jax.random.randint(key, (N_SEGMENT, SEQS), 1, LEN + 1)
    return drawn.at[:, 0].set(LEN).astype(jnp.int32)


def draw_lengths(key, part):
    return lengths_common(jax.random.fold_in(key, 11))


def draw_memory_lengths(key, part):
    return lengths_common(jax.random.fold_in(key, 12))


def shared_sets(key, shape, scale, limit):
    drawn = jnp.clip(jax.random.normal(key, (2,) + shape, jnp.float32) * scale, -limit, limit)
    return jnp.repeat(drawn, N_SEGMENT // 2, axis=0)


def draw_norm_gain(key, part):
    spread = shared_sets(jax.random.fold_in(key, 21), (3, D), 0.1, 0.5)
    return (1.0 + spread).astype(jnp.float32)


def draw_router(key, part):
    return shared_sets(jax.random.fold_in(key, 22), (D, EXPERTS), 2.0 / math.sqrt(D), 12.0 / math.sqrt(D)).astype(jnp.bfloat16)


def draw_w_in(key, part):
    return shared_sets(jax.random.fold_in(key, 23), (D, EXPERTS * FF), 1.0 / math.sqrt(D), 6.0 / math.sqrt(D)).astype(jnp.bfloat16)


def draw_w_out(key, part):
    return shared_sets(jax.random.fold_in(key, 24), (EXPERTS * FF, D), math.sqrt(2.0 / FF), 8.0 / math.sqrt(FF)).astype(jnp.bfloat16)


def plant(values, rng, smallest, largest):
    longest = values.shape.index(max(values.shape))
    spots = []
    for shift in (0, 1):
        where = [jax.random.randint(jax.random.fold_in(rng, axis), (), 0, length) for axis, length in enumerate(values.shape)]
        where[longest] = (where[longest] + shift) % values.shape[longest]
        spots.append(tuple(where))
    return values.at[spots[0]].set(smallest).at[spots[1]].set(largest)


def shard_levels(rng, dims, pieces, low, top_value):
    def one(position, shards_of):
        steps = jax.random.uniform(jax.random.fold_in(jax.random.fold_in(rng, 6), position), (shards_of,), jnp.float32, low / len(pieces), top_value / len(pieces))
        return jnp.repeat(jnp.exp(steps), dims[position] // shards_of).reshape((-1,) + (1,) * (len(dims) - position - 1))

    level = one(*pieces[0])
    for cut in pieces[1:]:
        level = level * one(*cut)
    return level


def deal_out(own_key, own, number, rows, count, top, most, skew):
    order = jax.random.permutation(own_key, count)
    heavy_load, usual = portions_of(count, rows * top, most, skew, True), portions_of(count, rows * top, most, skew, False)
    places = jnp.arange(count)

    def named(sizes, offset_by):
        used = int((sizes > 0).sum())
        fixed = max(1, used // 4)
        shifted = fixed + (places - fixed + offset_by * (used - fixed)) % max(1, count - fixed)
        return jnp.zeros((count,), jnp.int32).at[order[jnp.where(places < fixed, places, shifted)]].set(jnp.asarray(sizes, jnp.int32))

    sizes = jnp.where(number % 4 == 0, named(heavy_load, number // 4), named(usual, number - number // 4 - 1))
    mixed = jax.random.permutation(jax.random.fold_in(own, 3), count)
    giver, taker = mixed[0:count // 2 * 2:2], mixed[1:count // 2 * 2:2]
    slack = jnp.minimum(sizes[giver] - 1, most - sizes[taker]) // 2
    slack = jnp.where((giver == order[0]) | (taker == order[0]) | (sizes[taker] == 0), 0, jnp.maximum(slack, 0))
    shifted = jax.random.randint(jax.random.fold_in(own, 4), (count // 2,), 0, 1 << 20) % (slack + 1)
    sizes = sizes.at[giver].add(-shifted).at[taker].add(shifted)
    items = jnp.searchsorted(jnp.cumsum(sizes), jnp.arange(rows * top), side="right").astype(jnp.int32)
    grid = items.reshape(top, rows).T
    grid = grid[jax.random.permutation(jax.random.fold_in(own, 1), rows)]
    offset_by = jax.random.randint(jax.random.fold_in(own, 2), (rows, 1), 0, top)
    return jnp.take_along_axis(grid, (jnp.arange(top)[None, :] + offset_by) % top, axis=1)


def portions_of(number_of, total, bound, lean, full):
    weights = [(1 << 20) // math.isqrt(standing ** lean) + 1 for standing in range(1, number_of + 1)]
    largest = bound if full else min(bound, max(-(-total // number_of), total * weights[0] // sum(weights)))
    least = 1 if total - largest >= number_of - 1 else 0
    given, surplus = [largest] + [least] * (number_of - 1), total - largest - least * (number_of - 1)
    while surplus > 0:
        movable = [i for i in range(1, number_of) if given[i] < largest] or [i for i in range(1, number_of) if given[i] < bound]
        pool, remaining = sum([weights[i] for i in movable]), surplus
        for i in movable:
            more = min(bound - given[i], max(1, remaining * weights[i] // pool), surplus)
            given[i] = given[i] + more
            surplus = surplus - more
    return np.array(given)


def noise(rng, shape, deviation, bound, pieces=(), held_as=jnp.bfloat16):
    loudness = shard_levels(rng, shape, pieces, -0.22, 0.18) if pieces else 1.0
    values = jax.random.normal(rng, shape, jnp.float32) * deviation * loudness
    return jnp.minimum(jnp.maximum(values, -bound), bound).astype(held_as)


def setup_inputs(seed: int = 0) -> dict:
    seeds = jax.random.split(jax.random.key(seed), 13)
    hidden = noise(seeds[0], (N_SEGMENT, TOKENS, D), 1.0, 6.0, ((0, 2), (1, 16)))
    memory = noise(seeds[1], (N_SEGMENT, TOKENS, D), 1.0, 6.0, ((0, 2), (1, 16)))
    lengths = draw_lengths(jax.random.fold_in(seeds[12], 71), 0)
    memory_lengths = draw_memory_lengths(jax.random.fold_in(seeds[12], 71), 0)
    routes_keys = jax.random.split(jax.random.fold_in(seeds[4], 1), N_SEGMENT * TOKENS // TOK_DEV)
    routes_turns = jax.random.permutation(jax.random.fold_in(seeds[4], 3), N_SEGMENT * TOKENS // TOK_DEV)
    routes = jax.vmap(lambda own, number: deal_out(jax.random.fold_in(seeds[4], 2), own, number, TOK_DEV, EXPERTS, 2, CAP, 2))(routes_keys, routes_turns).reshape((N_SEGMENT, TOKENS, 2))
    norm_gain = draw_norm_gain(jax.random.fold_in(seeds[12], 71), 0)
    router = draw_router(jax.random.fold_in(seeds[12], 71), 0)
    w_in = draw_w_in(jax.random.fold_in(seeds[12], 71), 0)
    w_out = draw_w_out(jax.random.fold_in(seeds[12], 71), 0)
    shortlist = noise(seeds[9], (N_SEGMENT, D, VOCW), (D // 9) ** -0.5, 0.375, ((0, 2),))
    student = noise(seeds[10], (N_SEGMENT, TOKENS, VOCW), 3.0, 15.0, ((0, 2), (1, 16)), jnp.float32)
    targets = plant(jax.random.randint(seeds[11], (N_SEGMENT, TOKENS), 0, VOCW), jax.random.fold_in(seeds[11], 1), 0, VOCW - 1).astype(jnp.int32)
    return {"hidden": hidden, "memory": memory, "lengths": lengths, "memory_lengths": memory_lengths, "routes": routes, "norm_gain": norm_gain, "router": router, "w_in": w_in, "w_out": w_out, "shortlist": shortlist, "student": student, "targets": targets}


epsilon = 1e-05

def layer_norm(values, gain_row):
    centred = values - lax.optimization_barrier(jnp.mean(values, axis=-1, keepdims=True))
    spread = lax.optimization_barrier(jnp.mean(centred * centred, axis=-1, keepdims=True))
    return centred * lax.rsqrt(spread + epsilon) * gain_row

def round_trip(values):
    return lax.optimization_barrier(values.astype(jnp.bfloat16)).astype(jnp.float32)

def reference(hidden, memory, lengths, memory_lengths, routes, norm_gain, router, w_in, w_out, shortlist, student, targets):
    half_segments = N_SEGMENT // 2
    group_size = N_EXPERT // EXPERTS
    part_width = FF // group_size
    tokens = hidden.shape[1]
    positions = jnp.arange(tokens) % LEN
    seq_index = jnp.arange(tokens) // LEN
    expert_ids = jnp.arange(EXPERTS)
    score_scale = 1.0 / math.sqrt(HEAD_DIM)
    outputs = []
    loss_sum = jnp.zeros((), jnp.float32)
    loss_count = jnp.zeros((), jnp.float32)
    for section in range(N_SEGMENT):
        states = hidden[section].astype(jnp.float32)
        is_valid = positions < lengths[section][seq_index]
        if section >= half_segments:
            source = section - half_segments
            key_rows = memory[source]
            allowed = positions < memory_lengths[source][seq_index]
            queries = layer_norm(states, norm_gain[section, 0]).astype(jnp.bfloat16)
            query_heads = queries.reshape(SEQS, LEN, HEADS, HEAD_DIM).astype(jnp.float32)
            key_heads = key_rows.reshape(SEQS, LEN, HEADS, HEAD_DIM).astype(jnp.float32)
            scores = jnp.einsum('bqhd,bkhd->bhqk', query_heads, key_heads) * score_scale
            scores = jnp.where(allowed.reshape(SEQS, 1, 1, LEN), scores, -1e+30)
            weights = round_trip(jax.nn.softmax(scores, axis=-1))
            attended = jnp.einsum('bhqk,bkhd->bqhd', weights, key_heads).reshape(tokens, D)
            mid_states = states + attended
        else:
            mid_states = states
        normed = layer_norm(mid_states, norm_gain[section, 1]).astype(jnp.bfloat16)
        router_probs = jax.nn.softmax(jnp.dot(normed, router[section], preferred_element_type=jnp.float32), axis=-1)
        first_hot = (routes[section][:, 0:1] == expert_ids).astype(jnp.float32)
        second = (routes[section][:, 1:2] == expert_ids).astype(jnp.float32)
        prob_first = lax.optimization_barrier(jnp.sum(router_probs * first_hot, axis=-1, keepdims=True))
        prob_second = lax.optimization_barrier(jnp.sum(router_probs * second, axis=-1, keepdims=True))
        prob_total = prob_first + prob_second
        gate_rows = (prob_first * first_hot + prob_second * second) / prob_total
        combine_rows = gate_rows * is_valid[:, None].astype(jnp.float32)
        first_stack = w_in[section].reshape(D, EXPERTS, FF).transpose(1, 0, 2)
        second_stack = w_out[section].reshape(EXPERTS, group_size, part_width, D)

        def expert_step(running, stacked):
            first_weight, second_weight, share_col = stacked
            activated = jnp.maximum(jnp.dot(normed, first_weight, preferred_element_type=jnp.float32), 0.0)
            activated = round_trip(activated).reshape(tokens, group_size, part_width)
            parts = jnp.einsum('tgf,gfd->tgd', activated, second_weight.astype(jnp.float32))
            parts = round_trip(parts)
            return (running + share_col[:, None] * lax.optimization_barrier(jnp.sum(parts, axis=1)), None)
        moe_out, _ = lax.scan(expert_step, jnp.zeros((tokens, D), jnp.float32), (first_stack, second_stack, combine_rows.T))
        layer_out = (mid_states + moe_out).astype(jnp.bfloat16)
        outputs.append(layer_out)
        if section >= half_segments:
            final_normed = layer_norm(layer_out.astype(jnp.float32), norm_gain[section, 2]).astype(jnp.bfloat16)
            teacher = jax.nn.log_softmax(jnp.dot(final_normed, shortlist[section], preferred_element_type=jnp.float32), axis=-1)
            learner = jax.nn.log_softmax(student[section], axis=-1)
            picked = (targets[section][:, None] == jnp.arange(VOCW)).astype(jnp.float32)
            token_loss = lax.optimization_barrier(jnp.sum(jnp.exp(teacher) * (teacher - learner), axis=-1)) - lax.optimization_barrier(jnp.sum(picked * learner, axis=-1))
            counted = is_valid.astype(jnp.float32)
            loss_sum = loss_sum + jnp.sum(token_loss * counted)
            loss_count = loss_count + jnp.sum(counted)
    return (jnp.stack(outputs), loss_sum / loss_count)
```

```python
import functools
import math

import jax
import jax.numpy as jnp
from jax import lax
from jax.experimental import pallas as pl
from jax.experimental.pallas import tpu as pltpu
from jax.sharding import PartitionSpec as P

HEAD_DIM = 128
LEN = 32
EPS = 1e-05
MESH = pl.DeviceIdType.MESH
BF = jnp.bfloat16
F32 = jnp.float32


def layer_norm(values, gain_row):
    centred = values - jnp.mean(values, axis=-1, keepdims=True)
    spread = jnp.mean(centred * centred, axis=-1, keepdims=True)
    return centred * lax.rsqrt(spread + EPS) * gain_row


def xor(a, k, count):
    out = 0
    bit = 1
    while bit < count:
        out = out + lax.rem(a // bit + (k // bit) % 2, 2) * bit
        bit *= 2
    return out


def kernel(
    n_seg, n_exp, experts, gx, gc,
    hidden, memory, lengths, memory_lengths, routes, norm_gain, router,
    w_in, w_out, shortlist, student, targets,
    layer_out, loss_out,
    win, wout, short, kmem, klen_src, klen, mid,
    out_a, out_b, x, x_b, stage, act, y0,
    core_a, core_b, rc_a, rc_b, xs_a, xs_b, rx_a, rx_b, zs_a, zs_b, z_a, z_b, z_all, z_stage,
    lsend, lrecv, gsend, grecv,
    wsem, msem, ra, rb, sz, sx, sc, rc_s, rc_r, rx_s, rx_r, rz_s, rz_r, l_s, l_r, g_s, g_r,
):
    seg = lax.axis_index("segment")
    me = lax.axis_index("expert")
    half_seg = n_seg // 2
    group = gx * gc
    e = me // group
    j = lax.rem(me, group)
    xi = j // gc
    ci = lax.rem(j, gc)
    tok = hidden.shape[1]
    width = hidden.shape[2]
    heads = width // HEAD_DIM
    cap = 5 * tok // 8
    main = cap // 16 * 16
    rest = cap - main
    hop_order = [k for k in range(experts // 2, experts)] + [k for k in range(1, experts // 2)]

    def dev(e2, x2, c2):
        return (seg, (e2 * gx + x2) * gc + c2)

    loads = [
        pltpu.make_async_copy(w_in.at[0], win, wsem.at[0]),
        pltpu.make_async_copy(w_out.at[0], wout, wsem.at[1]),
        pltpu.make_async_copy(shortlist.at[0], short, wsem.at[2]),
    ]
    for load in loads:
        load.start()

    barrier = pltpu.get_barrier_semaphore()
    for d in range(1, n_exp):
        pl.semaphore_signal(
            barrier, inc=1, device_id=(seg, lax.rem(me + d, n_exp)), device_id_type=MESH
        )
    for d in range(1, n_seg):
        pl.semaphore_signal(
            barrier, inc=1, device_id=(lax.rem(seg + d, n_seg), me), device_id_type=MESH
        )
    klen_src[...] = jnp.broadcast_to(memory_lengths[0:1, 0:1], klen_src.shape)
    for q in range(1, tok // LEN):
        klen_src[q : q + 1, :] = jnp.broadcast_to(memory_lengths[0:1, q : q + 1], (1, 128))
    gains = norm_gain[0]
    states = hidden[0].astype(F32)
    pl.semaphore_wait(barrier, n_exp - 1 + n_seg - 1)

    is_decoder = seg >= half_seg
    to_seg = lax.rem(seg + half_seg, n_seg)
    mem_copy = pltpu.make_async_remote_copy(
        memory.at[0], kmem, msem.at[0], msem.at[1], device_id=(to_seg, me), device_id_type=MESH
    )
    len_copy = pltpu.make_async_remote_copy(
        klen_src, klen, msem.at[2], msem.at[3], device_id=(to_seg, me), device_id_type=MESH
    )

    @pl.when(seg < half_seg)
    def _():
        mem_copy.start()
        len_copy.start()
        mid[...] = states

    @pl.when(seg >= half_seg)
    def _():
        queries = layer_norm(states, gains[0:1]).astype(BF)
        len_copy.wait_recv()
        mem_copy.wait_recv()
        keys = kmem[...]
        col = lax.broadcasted_iota(jnp.int32, (tok, tok), 1)
        row = lax.broadcasted_iota(jnp.int32, (tok, tok), 0)
        klen_v = klen[...]
        allowed = jnp.zeros((tok, tok), jnp.bool_)
        for q in range(tok // LEN):
            inside = (col >= q * LEN) & (col - q * LEN < klen_v[q : q + 1, 0:1])
            inside = inside & (col < (q + 1) * LEN) & (row >= q * LEN) & (row < (q + 1) * LEN)
            allowed = allowed | inside
        scores = jnp.concatenate(
            [
                jnp.where(
                    allowed,
                    lax.dot_general(
                        queries[:, h * HEAD_DIM : (h + 1) * HEAD_DIM],
                        keys[:, h * HEAD_DIM : (h + 1) * HEAD_DIM],
                        (((1,), (1,)), ((), ())),
                        preferred_element_type=F32,
                    )
                    * (1.0 / math.sqrt(HEAD_DIM)),
                    -1e30,
                )
                for h in range(heads)
            ],
            axis=0,
        )
        top = jnp.max(scores, axis=-1, keepdims=True)
        raised = jnp.exp(scores - top)
        weights = (raised / jnp.sum(raised, axis=-1, keepdims=True)).astype(BF)
        for h in range(heads):
            part = slice(h * HEAD_DIM, (h + 1) * HEAD_DIM)
            mid[:, part] = states[:, part] + jnp.dot(
                weights[h * tok : (h + 1) * tok], keys[:, part], preferred_element_type=F32
            )

    normed = layer_norm(mid[...], gains[1:2]).astype(BF)

    expert_lane = lax.broadcasted_iota(jnp.int32, (tok, experts), 1)
    pos = lax.broadcasted_iota(jnp.int32, (tok, 1), 0)
    valid = jnp.zeros((tok, 1), F32)
    for q in range(tok // LEN):
        ok = (pos >= q * LEN) & (pos < (q + 1) * LEN) & (pos - q * LEN < lengths[0:1, q : q + 1])
        valid = valid + ok.astype(F32)
    route_pair = routes[0]
    first_hot = (route_pair[:, 0:1] == expert_lane).astype(F32)
    second_hot = (route_pair[:, 1:2] == expert_lane).astype(F32)
    chosen = (first_hot + second_hot) * valid
    before = (
        lax.broadcasted_iota(jnp.int32, (tok, tok), 1)
        < lax.broadcasted_iota(jnp.int32, (tok, tok), 0)
    ).astype(BF)
    rank = jnp.dot(before, chosen.astype(BF), preferred_element_type=F32)
    n_main = experts * main
    n_slots = experts * cap
    lanes = -(-n_slots // 128) * 128
    lane = lax.broadcasted_iota(jnp.int32, (1, lanes), 1)
    slot_of = jnp.full((1, lanes), -1, jnp.int32)
    expert_of = jnp.full((1, lanes), -1, jnp.int32)
    for k in range(experts):
        ek = xor(e, k, experts)
        in_main = (lane >= k * main) & (lane < (k + 1) * main)
        low = n_main + k * rest
        in_rest = (lane >= low) & (lane < low + rest)
        slot_of = jnp.where(in_main, lane - k * main, slot_of)
        slot_of = jnp.where(in_rest, lane - low + main, slot_of)
        expert_of = jnp.where(in_main | in_rest, ek, expert_of)
    placing = jnp.zeros((tok, lanes), F32)
    for k in range(experts):
        here = (expert_of == k) & (rank[:, k : k + 1] == slot_of.astype(F32))
        placing = placing + jnp.where(here, chosen[:, k : k + 1], 0.0)
    place_rows = jnp.transpose(placing)[0:n_slots].astype(BF)
    slots = jnp.dot(place_rows, normed, preferred_element_type=F32)

    def rows_a(dc, dx, k):
        return pl.ds(dc * gx * experts * cap + (dx * experts + k) * main, main)

    def index_b(dc, dx, k):
        return (dc * gx + dx) * experts + k

    x[rows_a(0, 0, 0), :] = slots[0:main].astype(BF)
    x_b[0] = slots[n_main : n_main + rest].astype(BF)
    for k in hop_order:
        out_a[k] = slots[k * main : (k + 1) * main].astype(BF)
        out_b[k] = slots[n_main + k * rest : n_main + (k + 1) * rest].astype(BF)

    waits = []

    def send(src, dst, s_sem, r_sem, target):
        copy = pltpu.make_async_remote_copy(
            src, dst, s_sem, r_sem, device_id=target, device_id_type=MESH
        )
        copy.start()
        waits.append(copy)

    def landed(ref, sem):
        pltpu.make_async_copy(ref, ref, sem).wait()

    def forward(slot_from, slot_to, sems, base, target):
        i, o = index_b(*slot_from), index_b(*slot_to)
        send(x.at[rows_a(*slot_from)], x.at[rows_a(*slot_to)], sems.at[base], ra.at[o], target)
        send(x_b.at[i], x_b.at[o], sems.at[base + 1], rb.at[o], target)

    for k in hop_order:
        target = dev(xor(e, k, experts), xi, ci)
        o = index_b(0, 0, k)
        send(out_a.at[k], x.at[rows_a(0, 0, k)], sz.at[2 * k], ra.at[o], target)
        send(out_b.at[k], x_b.at[o], sz.at[2 * k + 1], rb.at[o], target)

    core_dev = dev(e, xi, lax.rem(ci + 1, gc))
    for k in [0] + hop_order:
        if k:
            o = index_b(0, 0, k)
            landed(x.at[rows_a(0, 0, k)], ra.at[o])
            landed(x_b.at[o], rb.at[o])
        for d in range(1, gx):
            forward(
                (0, 0, k), (0, d, k), sx, 2 * ((d - 1) * experts + k),
                dev(e, lax.rem(xi + d, gx), ci),
            )
        forward((0, 0, k), (1, 0, k), sc, 2 * k, core_dev)
    for k in [0] + hop_order:
        for d in range(1, gx):
            o = index_b(0, d, k)
            landed(x.at[rows_a(0, d, k)], ra.at[o])
            landed(x_b.at[o], rb.at[o])
            forward((0, d, k), (1, d, k), sc, 2 * (d * experts + k), core_dev)
    for k in [0] + hop_order:
        for d in range(gx):
            o = index_b(1, d, k)
            landed(x.at[rows_a(1, d, k)], ra.at[o])
            landed(x_b.at[o], rb.at[o])

    blocks = gx * experts
    half_rows = blocks * cap
    half_main = blocks * main
    for dc in range(gc):
        for i in range(blocks):
            stage[i * rest : (i + 1) * rest, :] = x_b[dc * blocks + i].astype(F32)
        x[dc * half_rows + half_main : (dc + 1) * half_rows, :] = stage[...].astype(BF)

    units = win.shape[1]
    tile = min(256, units)
    loads[0].wait()

    @pl.loop(0, units // tile)
    def _(i):
        cols = pl.ds(pl.multiple_of(i * tile, tile), tile)
        act[:, cols] = jnp.maximum(
            jnp.dot(x[...], win[:, cols], preferred_element_type=F32), 0.0
        ).astype(BF)

    loads[1].wait()
    tile2 = 256

    @pl.loop(0, width // tile2)
    def _(i):
        cols = pl.ds(pl.multiple_of(i * tile2, tile2), tile2)
        part = jnp.dot(act[half_rows:, :], wout[:, cols], preferred_element_type=F32)
        core_a[:, cols] = part[0:half_main].astype(BF)
        for b in range(blocks):
            core_b[b, :, cols] = part[half_main + b * rest : half_main + (b + 1) * rest].astype(BF)

    send(core_a, rc_a, rc_s.at[0], rc_r.at[0], core_dev)
    send(core_b, rc_b, rc_s.at[1], rc_r.at[1], core_dev)

    @pl.loop(0, width // tile2)
    def _(i):
        cols = pl.ds(pl.multiple_of(i * tile2, tile2), tile2)
        y0[:, cols] = jnp.dot(act[0:half_rows, :], wout[:, cols], preferred_element_type=F32)

    landed(rc_a, rc_r.at[0])
    landed(rc_b, rc_r.at[1])

    def chip_sum(dx, k):
        b = dx * experts + k
        sum_a = y0[b * main : (b + 1) * main, :] + rc_a[b * main : (b + 1) * main, :].astype(F32)
        low = half_main + b * rest
        sum_b = y0[low : low + rest, :] + rc_b[b].astype(F32)
        return sum_a, sum_b

    back_order = hop_order + [0]
    for k in back_order:
        for d in range(1, gx):
            o = (d - 1) * experts + k
            sum_a, sum_b = chip_sum(d, k)
            xs_a[o] = sum_a.astype(BF)
            xs_b[o] = sum_b.astype(BF)
            target = dev(e, lax.rem(xi + gx - d, gx), ci)
            send(xs_a.at[o], rx_a.at[o], rx_s.at[2 * o], rx_r.at[2 * o], target)
            send(xs_b.at[o], rx_b.at[o], rx_s.at[2 * o + 1], rx_r.at[2 * o + 1], target)
    for k in back_order:
        sum_a, sum_b = chip_sum(0, k)
        for d in range(1, gx):
            o = (d - 1) * experts + k
            landed(rx_a.at[o], rx_r.at[2 * o])
            landed(rx_b.at[o], rx_r.at[2 * o + 1])
            sum_a = sum_a + rx_a[o].astype(F32)
            sum_b = sum_b + rx_b[o].astype(F32)
        if k:
            zs_a[k] = sum_a.astype(BF)
            zs_b[k] = sum_b.astype(BF)
            target = dev(xor(e, k, experts), xi, ci)
            send(zs_a.at[k], z_a.at[k], rz_s.at[2 * k], rz_r.at[2 * k], target)
            send(zs_b.at[k], z_b.at[k], rz_s.at[2 * k + 1], rz_r.at[2 * k + 1], target)
        else:
            z_all[0:main, :] = sum_a.astype(BF)
            z_stage[0:rest, :] = sum_b

    probs = jnp.dot(normed, router[0], preferred_element_type=F32)
    probs = jnp.exp(probs - jnp.max(probs, axis=-1, keepdims=True))
    probs = probs / jnp.sum(probs, axis=-1, keepdims=True)
    prob_first = jnp.sum(probs * first_hot, axis=-1, keepdims=True)
    prob_second = jnp.sum(probs * second_hot, axis=-1, keepdims=True)
    gate = (prob_first * first_hot + prob_second * second_hot) / (prob_first + prob_second)
    combine = jnp.zeros((tok, lanes), F32)
    for k in range(experts):
        combine = combine + jnp.where(expert_of == k, gate[:, k : k + 1], 0.0)
    combine = (combine * placing)[:, 0:n_slots]
    high = combine.astype(BF)
    low = (combine - high.astype(F32)).astype(BF)

    learner_in = student[0]
    shifted = learner_in - jnp.max(learner_in, axis=-1, keepdims=True)
    learner = shifted - jnp.log(jnp.sum(jnp.exp(shifted), axis=-1, keepdims=True))
    square = lax.broadcasted_iota(jnp.int32, (tok, tok), 0) == lax.broadcasted_iota(
        jnp.int32, (tok, tok), 1
    )
    target_col = jnp.sum(
        jnp.where(square, jnp.broadcast_to(targets[0:1, :], (tok, tok)), 0).astype(F32),
        axis=-1, keepdims=True,
    )
    vocab = student.shape[2]
    picked = lax.broadcasted_iota(jnp.int32, (tok, vocab), 1).astype(F32) == target_col
    hit = jnp.sum(jnp.where(picked, learner, 0.0), axis=-1, keepdims=True)
    loads[2].wait()

    for k in hop_order:
        landed(z_a.at[k], rz_r.at[2 * k])
        landed(z_b.at[k], rz_r.at[2 * k + 1])
        z_all[k * main : (k + 1) * main, :] = z_a[k]
        z_stage[k * rest : (k + 1) * rest, :] = z_b[k].astype(F32)
    z_all[n_main:, :] = z_stage[...].astype(BF)
    back = z_all[...]
    moe = jnp.dot(high, back, preferred_element_type=F32) + jnp.dot(
        low, back, preferred_element_type=F32
    )
    out = (mid[...] + moe).astype(BF)
    layer_out[0] = out

    final = layer_norm(out.astype(F32), gains[2:3]).astype(BF)
    logits = jnp.dot(final, short[...], preferred_element_type=F32)
    logits = logits - jnp.max(logits, axis=-1, keepdims=True)
    teacher = logits - jnp.log(jnp.sum(jnp.exp(logits), axis=-1, keepdims=True))
    token_loss = jnp.sum(jnp.exp(teacher) * (teacher - learner), axis=-1, keepdims=True) - hit
    counted = jnp.where(is_decoder, valid, 0.0)
    loss_sum = jnp.sum(token_loss * counted, axis=0, keepdims=True)
    loss_count = jnp.sum(counted, axis=0, keepdims=True)
    spot = lax.broadcasted_iota(jnp.int32, lsend.shape, 1)
    pair = jnp.where(spot == 0, loss_sum, jnp.where(spot == 1, loss_count, 0.0))
    lsend[...] = pair
    lrecv[me] = pair
    for d in range(1, n_exp):
        send(
            lsend, lrecv.at[me], l_s.at[d], l_r.at[d], (seg, lax.rem(me + d, n_exp))
        )
    for d in range(1, n_exp):
        landed(lrecv.at[lax.rem(me + n_exp - d, n_exp)], l_r.at[d])
    total = lrecv[0]
    for i in range(1, n_exp):
        total = total + lrecv[i]
    gsend[...] = total
    grecv[seg] = total
    for d in range(1, n_seg):
        send(
            gsend, grecv.at[seg], g_s.at[d], g_r.at[d], (lax.rem(seg + d, n_seg), me)
        )
    for d in range(1, n_seg):
        landed(grecv.at[lax.rem(seg + n_seg - d, n_seg)], g_r.at[d])
    total = grecv[0]
    for i in range(1, n_seg):
        total = total + grecv[i]
    loss_out[...] = total[0:1, 0:1] / total[0:1, 1:2]

    for copy in waits:
        copy.wait_send()

    @pl.when(seg < half_seg)
    def _():
        mem_copy.wait_send()
        len_copy.wait_send()


def local(
    hidden, memory, lengths, memory_lengths, routes, norm_gain, router,
    w_in, w_out, shortlist, student, targets,
):
    n_seg = lax.axis_size("segment")
    n_exp = lax.axis_size("expert")
    experts = router.shape[2]
    group = n_exp // experts
    gc = 2
    gx = group // gc
    tok, width = hidden.shape[1], hidden.shape[2]
    units = w_in.shape[2]
    vocab = shortlist.shape[2]
    cap = 5 * tok // 8
    main = cap // 16 * 16
    rest = cap - main
    blocks = gx * experts
    half_rows = blocks * cap
    vm = pl.BlockSpec(memory_space=pltpu.VMEM)
    hbm = pl.BlockSpec(memory_space=pl.ANY)
    v = pltpu.VMEM
    dma = pltpu.SemaphoreType.DMA
    nx = max(gx - 1, 1) * experts
    scratch = [
        v((width, units), BF), v((units, width), BF), v((width, vocab), BF),
        v((tok, width), BF), v((8, 128), jnp.int32), v((8, 128), jnp.int32), v((tok, width), F32),
        v((experts, main, width), BF), v((experts, rest, width), BF),
        v((gc * half_rows, width), BF), v((gc * blocks, rest, width), BF),
        v((blocks * rest, width), F32), v((gc * half_rows, units), BF), v((half_rows, width), F32),
        v((blocks * main, width), BF), v((blocks, rest, width), BF),
        v((blocks * main, width), BF), v((blocks, rest, width), BF),
        v((nx, main, width), BF), v((nx, rest, width), BF),
        v((nx, main, width), BF), v((nx, rest, width), BF),
        v((experts, main, width), BF), v((experts, rest, width), BF),
        v((experts, main, width), BF), v((experts, rest, width), BF),
        v((experts * cap, width), BF), v((experts * rest, width), F32),
        v((8, 128), F32), v((n_exp, 8, 128), F32), v((8, 128), F32), v((n_seg, 8, 128), F32),
        dma((3,)), dma((4,)), dma((gc * blocks,)), dma((gc * blocks,)),
        dma((2 * experts,)), dma((2 * nx,)), dma((2 * blocks,)),
        dma((2,)), dma((2,)), dma((2 * nx,)), dma((2 * nx,)),
        dma((2 * experts,)), dma((2 * experts,)),
        dma((n_exp,)), dma((n_exp,)), dma((n_seg,)), dma((n_seg,)),
    ]
    layer_out, loss = pl.pallas_call(
        functools.partial(kernel, n_seg, n_exp, experts, gx, gc),
        out_shape=(
            jax.ShapeDtypeStruct((1, tok, width), BF),
            jax.ShapeDtypeStruct((1, 1), F32),
        ),
        in_specs=[vm, hbm, vm, vm, vm, vm, vm, hbm, hbm, hbm, vm, vm],
        out_specs=(vm, vm),
        scratch_shapes=scratch,
        compiler_params=pltpu.CompilerParams(
            collective_id=0, has_side_effects=True, vmem_limit_bytes=60 * 1024 * 1024
        ),
    )(
        hidden, memory, lengths, memory_lengths, routes, norm_gain, router,
        w_in, w_out, shortlist, student, targets,
    )
    return layer_out, loss[0, 0]


def solution(mesh):
    placed = (
        P("segment", "expert", None),
        P("segment", "expert", None),
        P("segment", "expert"),
        P("segment", "expert"),
        P("segment", "expert", None),
        P("segment", None, None),
        P("segment", None, None),
        P("segment", None, "expert"),
        P("segment", "expert", None),
        P("segment", None, None),
        P("segment", "expert", None),
        P("segment", "expert"),
    )
    return jax.shard_map(
        local,
        mesh=mesh,
        in_specs=placed,
        out_specs=(P("segment", "expert", None), P()),
        check_vma=False,
    )
```

```python
import functools
import math

import jax
import jax.numpy as jnp
from jax import lax
from jax.experimental import pallas as pl
from jax.experimental.pallas import tpu as pltpu
from jax.sharding import PartitionSpec as P

HEAD_DIM = 128
LEN = 32
EPS = 1e-05
MESH = pl.DeviceIdType.MESH
BF = jnp.bfloat16
F32 = jnp.float32


def layer_norm(values, gain_row):
    centred = values - jnp.mean(values, axis=-1, keepdims=True)
    spread = jnp.mean(centred * centred, axis=-1, keepdims=True)
    return centred * lax.rsqrt(spread + EPS) * gain_row


def xor(a, k, count):
    out = 0
    bit = 1
    while bit < count:
        out = out + lax.rem(a // bit + (k // bit) % 2, 2) * bit
        bit *= 2
    return out


def kernel(
    n_seg, n_exp, experts, gx, gc,
    hidden_any, memory, lengths, memory_lengths, routes_any, gain_any, router_any,
    w_in, w_out, shortlist, student_any, targets,
    layer_out, loss_out,
    hidden, routes, norm_gain, router, student, out_stage,
    win, wout, short, kmem, klen_src, klen, mid,
    out_a, out_b, x, x_b, stage, act, y0,
    core_a, core_b, rc_a, rc_b, xs_a, xs_b, rx_a, rx_b, zs_a, zs_b, z_a, z_b, z_all, z_stage,
    lsend, lrecv,
    wsem, msem, ra, sz, sx, sc, rc_s, rc_r, rx_s, rx_r, rz_s, rz_r, l_s, l_r,
):
    seg = lax.axis_index("segment")
    me = lax.axis_index("expert")
    half_seg = n_seg // 2
    group = gx * gc
    e = me // group
    j = lax.rem(me, group)
    xi = j // gc
    ci = lax.rem(j, gc)
    tok = hidden.shape[1]
    width = hidden.shape[2]
    heads = width // HEAD_DIM
    cap = 5 * tok // 8
    main = cap // 16 * 16
    rest = cap - main
    hop_order = [k for k in range(experts // 2, experts)] + [k for k in range(1, experts // 2)]

    def peer(ds, d):
        return (lax.rem(seg + ds, n_seg), lax.rem(me + d, n_exp))

    def dev(e2, x2, c2):
        return (seg, (e2 * gx + x2) * gc + c2)

    barrier = pltpu.get_barrier_semaphore()
    for ds in range(n_seg):
        for d in range(n_exp):
            if ds or d:
                pl.semaphore_signal(
                    barrier, inc=1, device_id=peer(ds, d), device_id_type=MESH
                )

    early = [
        pltpu.make_async_copy(hidden_any, hidden, wsem.at[3]),
        pltpu.make_async_copy(gain_any, norm_gain, wsem.at[4]),
        pltpu.make_async_copy(routes_any, routes, wsem.at[5]),
        pltpu.make_async_copy(router_any, router, wsem.at[6]),
        pltpu.make_async_copy(student_any, student, wsem.at[7]),
    ]
    for load in early:
        load.start()
    loads = [
        pltpu.make_async_copy(w_in.at[0], win, wsem.at[0]),
        pltpu.make_async_copy(w_out.at[0], wout, wsem.at[1]),
        pltpu.make_async_copy(shortlist.at[0], short, wsem.at[2]),
    ]
    for load in loads:
        load.start()

    klen_src[...] = jnp.broadcast_to(memory_lengths[0:1, 0:1], klen_src.shape)
    for q in range(1, tok // LEN):
        klen_src[q : q + 1, :] = jnp.broadcast_to(memory_lengths[0:1, q : q + 1], (1, 128))
    early[0].wait()
    early[1].wait()
    gains = [norm_gain[i] for i in range(3)]
    states = hidden[0].astype(F32)
    pl.semaphore_wait(barrier, n_exp * n_seg - 1)

    is_decoder = seg >= half_seg
    to_seg = lax.rem(seg + half_seg, n_seg)
    mem_copy = pltpu.make_async_remote_copy(
        memory.at[0], kmem, msem.at[0], msem.at[1], device_id=(to_seg, me), device_id_type=MESH
    )
    len_copy = pltpu.make_async_remote_copy(
        klen_src, klen, msem.at[2], msem.at[3], device_id=(to_seg, me), device_id_type=MESH
    )

    @pl.when(seg < half_seg)
    def _():
        mem_copy.start()
        len_copy.start()
        mid[...] = states

    @pl.when(seg >= half_seg)
    def _():
        queries = layer_norm(states, gains[0]).astype(BF)
        len_copy.wait_recv()
        mem_copy.wait_recv()
        keys = kmem[...]
        col = lax.broadcasted_iota(jnp.int32, (tok, tok), 1)
        row = lax.broadcasted_iota(jnp.int32, (tok, tok), 0)
        klen_v = klen[...]
        allowed = jnp.zeros((tok, tok), jnp.bool_)
        for q in range(tok // LEN):
            inside = (col >= q * LEN) & (col - q * LEN < klen_v[q : q + 1, 0:1])
            inside = inside & (col < (q + 1) * LEN) & (row >= q * LEN) & (row < (q + 1) * LEN)
            allowed = allowed | inside
        scores = jnp.concatenate(
            [
                jnp.where(
                    allowed,
                    lax.dot_general(
                        queries[:, h * HEAD_DIM : (h + 1) * HEAD_DIM],
                        keys[:, h * HEAD_DIM : (h + 1) * HEAD_DIM],
                        (((1,), (1,)), ((), ())),
                        preferred_element_type=F32,
                    )
                    * (1.0 / math.sqrt(HEAD_DIM)),
                    -1e30,
                )
                for h in range(heads)
            ],
            axis=0,
        )
        top = jnp.max(scores, axis=-1, keepdims=True)
        raised = jnp.exp(scores - top)
        weights = (raised / jnp.sum(raised, axis=-1, keepdims=True)).astype(BF)
        for h in range(heads):
            part = slice(h * HEAD_DIM, (h + 1) * HEAD_DIM)
            mid[:, part] = states[:, part] + jnp.dot(
                weights[h * tok : (h + 1) * tok], keys[:, part], preferred_element_type=F32
            )

    normed = layer_norm(mid[...], gains[1]).astype(BF)

    early[2].wait()
    expert_lane = lax.broadcasted_iota(jnp.int32, (tok, experts), 1)
    pos = lax.broadcasted_iota(jnp.int32, (tok, 1), 0)
    valid = jnp.zeros((tok, 1), F32)
    for q in range(tok // LEN):
        ok = (pos >= q * LEN) & (pos < (q + 1) * LEN) & (pos - q * LEN < lengths[0:1, q : q + 1])
        valid = valid + ok.astype(F32)
    square = lax.broadcasted_iota(jnp.int32, (tok, tok), 0) == lax.broadcasted_iota(
        jnp.int32, (tok, tok), 1
    )

    def column(row):
        spread = jnp.where(square, jnp.broadcast_to(row, (tok, tok)), 0)
        return jnp.sum(spread.astype(F32), axis=-1, keepdims=True)

    expert_lane = expert_lane.astype(F32)
    first_hot = (column(routes[0, 0:1, :]) == expert_lane).astype(F32)
    second_hot = (column(routes[0, 1:2, :]) == expert_lane).astype(F32)
    chosen = (first_hot + second_hot) * valid
    before = (
        lax.broadcasted_iota(jnp.int32, (tok, tok), 1)
        < lax.broadcasted_iota(jnp.int32, (tok, tok), 0)
    ).astype(BF)
    rank = jnp.dot(before, chosen.astype(BF), preferred_element_type=F32)
    n_main = experts * main
    n_slots = experts * cap
    lanes = -(-n_slots // 128) * 128
    lane = lax.broadcasted_iota(jnp.int32, (1, lanes), 1)
    slot_of = jnp.full((1, lanes), -1, jnp.int32)
    expert_of = jnp.full((1, lanes), -1, jnp.int32)
    for k in range(experts):
        ek = xor(e, k, experts)
        in_main = (lane >= k * main) & (lane < (k + 1) * main)
        low = n_main + k * rest
        in_rest = (lane >= low) & (lane < low + rest)
        slot_of = jnp.where(in_main, lane - k * main, slot_of)
        slot_of = jnp.where(in_rest, lane - low + main, slot_of)
        expert_of = jnp.where(in_main | in_rest, ek, expert_of)
    placing = jnp.zeros((tok, lanes), F32)
    for k in range(experts):
        here = (expert_of == k) & (rank[:, k : k + 1] == slot_of.astype(F32))
        placing = placing + jnp.where(here, chosen[:, k : k + 1], 0.0)
    place_rows = jnp.transpose(placing)[0:n_slots].astype(BF)
    slots = jnp.dot(place_rows, normed, preferred_element_type=F32)

    def rows_a(dc, dx, k):
        return pl.ds(dc * gx * experts * cap + (dx * experts + k) * main, main)

    def index_b(dc, dx, k):
        return (dc * gx + dx) * experts + k

    x[rows_a(0, 0, 0), :] = slots[0:main].astype(BF)
    x_b[0] = slots[n_main : n_main + rest].astype(BF)
    for k in hop_order:
        out_a[k] = slots[k * main : (k + 1) * main].astype(BF)
        out_b[k] = slots[n_main + k * rest : n_main + (k + 1) * rest].astype(BF)

    waits = []

    def send(src, dst, s_sem, r_sem, target):
        copy = pltpu.make_async_remote_copy(
            src, dst, s_sem, r_sem, device_id=target, device_id_type=MESH
        )
        copy.start()
        waits.append(copy)

    def landed(ref, sem):
        pltpu.make_async_copy(ref, ref, sem).wait()

    half_width = width // 2

    def piece(slot, p):
        if p < 2:
            return x.at[rows_a(*slot), p * half_width : (p + 1) * half_width]
        return x_b.at[index_b(*slot)]

    def arrived(slot, p):
        landed(piece(slot, p), ra.at[3 * index_b(*slot) + p])

    def forward(slot_from, slot_to, p, sems, base, target):
        send(
            piece(slot_from, p), piece(slot_to, p), sems.at[3 * base + p],
            ra.at[3 * index_b(*slot_to) + p], target,
        )

    for k in hop_order:
        target = dev(xor(e, k, experts), xi, ci)
        for p in range(3):
            src = out_a.at[k, :, p * half_width : (p + 1) * half_width] if p < 2 else out_b.at[k]
            send(
                src, piece((0, 0, k), p), sz.at[3 * k + p], ra.at[3 * index_b(0, 0, k) + p], target
            )

    core_dev = dev(e, xi, lax.rem(ci + 1, gc))

    def from_column(k):
        for p in range(3):
            if k:
                arrived((0, 0, k), p)
            for d in range(1, gx):
                forward(
                    (0, 0, k), (0, d, k), p, sx, (d - 1) * experts + k,
                    dev(e, lax.rem(xi + d, gx), ci),
                )
            forward((0, 0, k), (1, 0, k), p, sc, k, core_dev)

    def from_chips(k):
        for p in range(3):
            for d in range(1, gx):
                arrived((0, d, k), p)
                forward((0, d, k), (1, d, k), p, sc, d * experts + k, core_dev)

    order = [0] + hop_order
    for i, k in enumerate(order):
        from_column(k)
        if i:
            from_chips(order[i - 1])
    from_chips(order[-1])
    for k in order:
        for d in range(gx):
            for p in range(3):
                arrived((1, d, k), p)

    blocks = gx * experts
    half_rows = blocks * cap
    half_main = blocks * main
    for dc in range(gc):
        for i in range(blocks):
            stage[i * rest : (i + 1) * rest, :] = x_b[dc * blocks + i].astype(F32)
        x[dc * half_rows + half_main : (dc + 1) * half_rows, :] = stage[...].astype(BF)

    units = win.shape[1]
    tile = min(256, units)
    loads[0].wait()

    @pl.loop(0, units // tile)
    def _(i):
        cols = pl.ds(pl.multiple_of(i * tile, tile), tile)
        act[:, cols] = jnp.maximum(
            jnp.dot(x[...], win[:, cols], preferred_element_type=F32), 0.0
        ).astype(BF)

    loads[1].wait()
    tile2 = 256

    @pl.loop(0, width // tile2)
    def _(i):
        cols = pl.ds(pl.multiple_of(i * tile2, tile2), tile2)
        part = jnp.dot(act[half_rows:, :], wout[:, cols], preferred_element_type=F32)
        core_a[:, cols] = part[0:half_main].astype(BF)
        for b in range(blocks):
            core_b[b, :, cols] = part[half_main + b * rest : half_main + (b + 1) * rest].astype(BF)

    send(core_a, rc_a, rc_s.at[0], rc_r.at[0], core_dev)
    send(core_b, rc_b, rc_s.at[1], rc_r.at[1], core_dev)

    @pl.loop(0, width // tile2)
    def _(i):
        cols = pl.ds(pl.multiple_of(i * tile2, tile2), tile2)
        y0[:, cols] = jnp.dot(act[0:half_rows, :], wout[:, cols], preferred_element_type=F32)

    landed(rc_a, rc_r.at[0])
    landed(rc_b, rc_r.at[1])

    def chip_sum(dx, k):
        b = dx * experts + k
        sum_a = y0[b * main : (b + 1) * main, :] + rc_a[b * main : (b + 1) * main, :].astype(F32)
        low = half_main + b * rest
        sum_b = y0[low : low + rest, :] + rc_b[b].astype(F32)
        return sum_a, sum_b

    back_order = hop_order + [0]
    for k in back_order:
        for d in range(1, gx):
            o = (d - 1) * experts + k
            sum_a, sum_b = chip_sum(d, k)
            xs_a[o] = sum_a.astype(BF)
            xs_b[o] = sum_b.astype(BF)
            target = dev(e, lax.rem(xi + gx - d, gx), ci)
            send(xs_a.at[o], rx_a.at[o], rx_s.at[2 * o], rx_r.at[2 * o], target)
            send(xs_b.at[o], rx_b.at[o], rx_s.at[2 * o + 1], rx_r.at[2 * o + 1], target)
    for k in back_order:
        sum_a, sum_b = chip_sum(0, k)
        for d in range(1, gx):
            o = (d - 1) * experts + k
            landed(rx_a.at[o], rx_r.at[2 * o])
            landed(rx_b.at[o], rx_r.at[2 * o + 1])
            sum_a = sum_a + rx_a[o].astype(F32)
            sum_b = sum_b + rx_b[o].astype(F32)
        if k:
            zs_a[k] = sum_a.astype(BF)
            zs_b[k] = sum_b.astype(BF)
            target = dev(xor(e, k, experts), xi, ci)
            send(zs_a.at[k], z_a.at[k], rz_s.at[2 * k], rz_r.at[2 * k], target)
            send(zs_b.at[k], z_b.at[k], rz_s.at[2 * k + 1], rz_r.at[2 * k + 1], target)
        else:
            z_all[0:main, :] = sum_a.astype(BF)
            z_stage[0:rest, :] = sum_b

    early[3].wait()
    probs = lax.dot_general(
        normed, router[0], (((1,), (1,)), ((), ())), preferred_element_type=F32
    )
    probs = jnp.exp(probs - jnp.max(probs, axis=-1, keepdims=True))
    probs = probs / jnp.sum(probs, axis=-1, keepdims=True)
    prob_first = jnp.sum(probs * first_hot, axis=-1, keepdims=True)
    prob_second = jnp.sum(probs * second_hot, axis=-1, keepdims=True)
    gate = (prob_first * first_hot + prob_second * second_hot) / (prob_first + prob_second)
    combine = jnp.zeros((tok, lanes), F32)
    for k in range(experts):
        combine = combine + jnp.where(expert_of == k, gate[:, k : k + 1], 0.0)
    combine = (combine * placing)[:, 0:n_slots]
    high = combine.astype(BF)
    low = (combine - high.astype(F32)).astype(BF)

    early[4].wait()
    learner_in = student[0]
    shifted = learner_in - jnp.max(learner_in, axis=-1, keepdims=True)
    learner = shifted - jnp.log(jnp.sum(jnp.exp(shifted), axis=-1, keepdims=True))
    target_col = column(targets[0:1, :])
    vocab = student.shape[2]
    picked = lax.broadcasted_iota(jnp.int32, (tok, vocab), 1).astype(F32) == target_col
    hit = jnp.sum(jnp.where(picked, learner, 0.0), axis=-1, keepdims=True)
    loads[2].wait()

    for k in hop_order:
        landed(z_a.at[k], rz_r.at[2 * k])
        landed(z_b.at[k], rz_r.at[2 * k + 1])
        z_all[k * main : (k + 1) * main, :] = z_a[k]
        z_stage[k * rest : (k + 1) * rest, :] = z_b[k].astype(F32)
    z_all[n_main:, :] = z_stage[...].astype(BF)
    back = z_all[...]
    moe = jnp.dot(high, back, preferred_element_type=F32) + jnp.dot(
        low, back, preferred_element_type=F32
    )
    out = (mid[...] + moe).astype(BF)
    out_stage[...] = out
    out_copy = pltpu.make_async_copy(out_stage, layer_out.at[0], wsem.at[8])
    out_copy.start()

    final = layer_norm(out.astype(F32), gains[2]).astype(BF)
    logits = jnp.dot(final, short[...], preferred_element_type=F32)
    logits = logits - jnp.max(logits, axis=-1, keepdims=True)
    teacher = logits - jnp.log(jnp.sum(jnp.exp(logits), axis=-1, keepdims=True))
    token_loss = jnp.sum(jnp.exp(teacher) * (teacher - learner), axis=-1, keepdims=True) - hit
    counted = jnp.where(is_decoder, valid, 0.0)
    loss_sum = jnp.sum(token_loss * counted, axis=0, keepdims=True)
    loss_count = jnp.sum(counted, axis=0, keepdims=True)
    spot = lax.broadcasted_iota(jnp.int32, lsend.shape, 1)
    pair = jnp.where(spot == 0, loss_sum, jnp.where(spot == 1, loss_count, 0.0))
    lsend[...] = pair

    @pl.when(is_decoder)
    def _():
        mine = (seg - half_seg) * n_exp
        lrecv[mine + me] = pair
        for ds in range(n_seg):
            for d in range(n_exp):
                if ds or d:
                    pltpu.make_async_remote_copy(
                        lsend, lrecv.at[mine + me], l_s.at[ds * n_exp + d], l_r.at[mine + d],
                        device_id=peer(ds, d), device_id_type=MESH,
                    ).start()

    for q in range(n_seg - half_seg):
        for d in range(n_exp):
            source = q * n_exp + lax.rem(me + n_exp - d, n_exp)
            if d:
                landed(lrecv.at[source], l_r.at[q * n_exp + d])
            else:
                @pl.when(seg != q + half_seg)
                def _():
                    landed(lrecv.at[source], l_r.at[q * n_exp])

    total = lrecv[0]
    for i in range(1, (n_seg - half_seg) * n_exp):
        total = total + lrecv[i]
    loss_out[...] = total[0:1, 0:1] / total[0:1, 1:2]

    @pl.when(is_decoder)
    def _():
        for i in range(1, n_seg * n_exp):
            pltpu.make_async_copy(lsend, lsend, l_s.at[i]).wait()

    out_copy.wait()
    for copy in waits:
        copy.wait_send()

    @pl.when(seg < half_seg)
    def _():
        mem_copy.wait_send()
        len_copy.wait_send()


def local(
    hidden, memory, lengths, memory_lengths, routes, norm_gain, router,
    w_in, w_out, shortlist, student, targets,
):
    n_seg = lax.axis_size("segment")
    n_exp = lax.axis_size("expert")
    experts = router.shape[2]
    group = n_exp // experts
    gc = 2
    gx = group // gc
    tok, width = hidden.shape[1], hidden.shape[2]
    units = w_in.shape[2]
    vocab = shortlist.shape[2]
    cap = 5 * tok // 8
    main = cap // 16 * 16
    rest = cap - main
    blocks = gx * experts
    half_rows = blocks * cap
    vm = pl.BlockSpec(memory_space=pltpu.VMEM)
    hbm = pl.BlockSpec(memory_space=pl.ANY)
    v = pltpu.VMEM
    dma = pltpu.SemaphoreType.DMA
    nx = max(gx - 1, 1) * experts
    scratch = [
        v((1, tok, width), BF), v((1, 2, tok), jnp.int32), v((3, 1, width), F32),
        v((1, experts, width), BF), v((1, tok, vocab), F32), v((tok, width), BF),
        v((width, units), BF), v((units, width), BF), v((width, vocab), BF),
        v((tok, width), BF), v((8, 128), jnp.int32), v((8, 128), jnp.int32), v((tok, width), F32),
        v((experts, main, width), BF), v((experts, rest, width), BF),
        v((gc * half_rows, width), BF), v((gc * blocks, rest, width), BF),
        v((blocks * rest, width), F32), v((gc * half_rows, units), BF), v((half_rows, width), F32),
        v((blocks * main, width), BF), v((blocks, rest, width), BF),
        v((blocks * main, width), BF), v((blocks, rest, width), BF),
        v((nx, main, width), BF), v((nx, rest, width), BF),
        v((nx, main, width), BF), v((nx, rest, width), BF),
        v((experts, main, width), BF), v((experts, rest, width), BF),
        v((experts, main, width), BF), v((experts, rest, width), BF),
        v((experts * cap, width), BF), v((experts * rest, width), F32),
        v((8, 128), F32), v(((n_seg - n_seg // 2) * n_exp, 8, 128), F32),
        dma((9,)), dma((4,)), dma((3 * gc * blocks,)),
        dma((3 * experts,)), dma((3 * nx,)), dma((3 * blocks,)),
        dma((2,)), dma((2,)), dma((2 * nx,)), dma((2 * nx,)),
        dma((2 * experts,)), dma((2 * experts,)),
        dma((n_seg * n_exp,)), dma(((n_seg - n_seg // 2) * n_exp,)),
    ]
    layer_out, loss = pl.pallas_call(
        functools.partial(kernel, n_seg, n_exp, experts, gx, gc),
        out_shape=(
            jax.ShapeDtypeStruct((1, tok, width), BF),
            jax.ShapeDtypeStruct((1, 1), F32),
        ),
        in_specs=[hbm, hbm, vm, vm, hbm, hbm, hbm, hbm, hbm, hbm, hbm, vm],
        out_specs=(hbm, vm),
        scratch_shapes=scratch,
        compiler_params=pltpu.CompilerParams(
            collective_id=0, has_side_effects=True, vmem_limit_bytes=60 * 1024 * 1024
        ),
    )(
        hidden, memory, lengths, memory_lengths, jnp.swapaxes(routes, 1, 2),
        jnp.swapaxes(norm_gain, 0, 1), jnp.swapaxes(router, 1, 2),
        w_in, w_out, shortlist, student, targets,
    )
    return layer_out, loss[0, 0]


def solution(mesh):
    placed = (
        P("segment", "expert", None),
        P("segment", "expert", None),
        P("segment", "expert"),
        P("segment", "expert"),
        P("segment", "expert", None),
        P("segment", None, None),
        P("segment", None, None),
        P("segment", None, "expert"),
        P("segment", "expert", None),
        P("segment", None, None),
        P("segment", "expert", None),
        P("segment", "expert"),
    )
    return jax.shard_map(
        local,
        mesh=mesh,
        in_specs=placed,
        out_specs=(P("segment", "expert", None), P()),
        check_vma=False,
    )
```

```python
import functools
import math

import jax
import jax.numpy as jnp
from jax import lax
from jax.experimental import pallas as pl
from jax.experimental.pallas import tpu as pltpu
from jax.sharding import PartitionSpec as P

HEAD_DIM = 128
LEN = 32
EPS = 1e-05
MESH = pl.DeviceIdType.MESH
BF = jnp.bfloat16
F32 = jnp.float32


def layer_norm(values, gain_row):
    centred = values - jnp.mean(values, axis=-1, keepdims=True)
    spread = jnp.mean(centred * centred, axis=-1, keepdims=True)
    return centred * lax.rsqrt(spread + EPS) * gain_row


def xor(a, k, count):
    out = 0
    bit = 1
    while bit < count:
        out = out + lax.rem(a // bit + (k // bit) % 2, 2) * bit
        bit *= 2
    return out


def kernel(
    n_seg, n_exp, experts, gx, gc,
    hidden_any, memory, lengths, memory_lengths, routes_any, gain_any, router_any,
    w_in, w_out, shortlist, student_any, targets,
    layer_out, loss_out,
    hidden, routes, norm_gain, router, student, out_stage,
    win, wout, short, kmem, klen_src, klen, mid,
    out_a, out_b, x, x_b, stage, act, y0,
    core_a, core_b, rc_a, rc_b, xs_a, xs_b, rx_a, rx_b, zs_a, zs_b, z_a, z_b, z_all, z_stage,
    lsend, lrecv,
    wsem, msem, ra, sz, sx, sc, rc_s, rc_r, rx_s, rx_r, rz_s, rz_r, l_s, l_r,
):
    seg = lax.axis_index("segment")
    me = lax.axis_index("expert")
    half_seg = n_seg // 2
    group = gx * gc
    e = me // group
    j = lax.rem(me, group)
    xi = j // gc
    ci = lax.rem(j, gc)
    tok = hidden.shape[1]
    width = hidden.shape[2]
    heads = width // HEAD_DIM
    cap = 5 * tok // 8
    main = cap // 16 * 16
    rest = cap - main
    hop_order = list(range(experts - 1, 0, -1))
    back_order = hop_order + [0]
    span = experts // 2
    turns = [back_order[0:span], back_order[span:]]
    chunk_main = gx * span * main
    chunk = gx * span * cap

    def peer(ds, d):
        return (lax.rem(seg + ds, n_seg), lax.rem(me + d, n_exp))

    def dev(e2, x2, c2):
        return (seg, (e2 * gx + x2) * gc + c2)

    barrier = pltpu.get_barrier_semaphore()
    for ds in range(n_seg):
        for d in range(n_exp):
            if ds or d:
                pl.semaphore_signal(
                    barrier, inc=1, device_id=peer(ds, d), device_id_type=MESH
                )

    early = [
        pltpu.make_async_copy(hidden_any, hidden, wsem.at[3]),
        pltpu.make_async_copy(gain_any, norm_gain, wsem.at[4]),
        pltpu.make_async_copy(routes_any, routes, wsem.at[5]),
        pltpu.make_async_copy(router_any, router, wsem.at[6]),
        pltpu.make_async_copy(student_any, student, wsem.at[7]),
    ]
    for load in early:
        load.start()
    loads = [
        pltpu.make_async_copy(w_in.at[0], win, wsem.at[0]),
        pltpu.make_async_copy(w_out.at[0], wout, wsem.at[1]),
        pltpu.make_async_copy(shortlist.at[0], short, wsem.at[2]),
    ]
    for load in loads:
        load.start()

    klen_src[...] = jnp.broadcast_to(memory_lengths[0:1, 0:1], klen_src.shape)
    for q in range(1, tok // LEN):
        klen_src[q : q + 1, :] = jnp.broadcast_to(memory_lengths[0:1, q : q + 1], (1, 128))
    early[0].wait()
    early[1].wait()
    gains = [norm_gain[i] for i in range(3)]
    states = hidden[0].astype(F32)
    pl.semaphore_wait(barrier, n_exp * n_seg - 1)

    is_decoder = seg >= half_seg
    to_seg = lax.rem(seg + half_seg, n_seg)
    mem_parts = 4 if heads % 4 == 0 else 1
    mem_width = width // mem_parts
    mem_copies = []
    for p in range(mem_parts):
        part = slice(p * mem_width, (p + 1) * mem_width)
        mem_copies.append(
            pltpu.make_async_remote_copy(
                memory.at[0, :, part], kmem.at[:, part], msem.at[2 + p], msem.at[6 + p],
                device_id=(to_seg, me), device_id_type=MESH,
            )
        )
    len_copy = pltpu.make_async_remote_copy(
        klen_src, klen, msem.at[0], msem.at[1], device_id=(to_seg, me), device_id_type=MESH
    )

    @pl.when(seg < half_seg)
    def _():
        len_copy.start()
        for copy in mem_copies:
            copy.start()
        mid[...] = states

    @pl.when(seg >= half_seg)
    def _():
        queries = layer_norm(states, gains[0]).astype(BF)
        len_copy.wait_recv()
        col = lax.broadcasted_iota(jnp.int32, (tok, tok), 1)
        row = lax.broadcasted_iota(jnp.int32, (tok, tok), 0)
        klen_v = klen[...]
        allowed = jnp.zeros((tok, tok), jnp.bool_)
        for q in range(tok // LEN):
            inside = (col >= q * LEN) & (col - q * LEN < klen_v[q : q + 1, 0:1])
            inside = inside & (col < (q + 1) * LEN) & (row >= q * LEN) & (row < (q + 1) * LEN)
            allowed = allowed | inside
        for p in range(mem_parts):
            mem_copies[p].wait_recv()
            span_heads = range(p * heads // mem_parts, (p + 1) * heads // mem_parts)
            parts = [slice(h * HEAD_DIM, (h + 1) * HEAD_DIM) for h in span_heads]
            scores = jnp.concatenate(
                [
                    jnp.where(
                        allowed,
                        lax.dot_general(
                            queries[:, part], kmem[:, part], (((1,), (1,)), ((), ())),
                            preferred_element_type=F32,
                        )
                        * (1.0 / math.sqrt(HEAD_DIM)),
                        -1e30,
                    )
                    for part in parts
                ],
                axis=0,
            )
            top = jnp.max(scores, axis=-1, keepdims=True)
            raised = jnp.exp(scores - top)
            weights = (raised / jnp.sum(raised, axis=-1, keepdims=True)).astype(BF)
            for i, part in enumerate(parts):
                mid[:, part] = states[:, part] + jnp.dot(
                    weights[i * tok : (i + 1) * tok], kmem[:, part], preferred_element_type=F32
                )

    normed = layer_norm(mid[...], gains[1]).astype(BF)

    early[2].wait()
    expert_lane = lax.broadcasted_iota(jnp.int32, (tok, experts), 1)
    pos = lax.broadcasted_iota(jnp.int32, (tok, 1), 0)
    valid = jnp.zeros((tok, 1), F32)
    for q in range(tok // LEN):
        ok = (pos >= q * LEN) & (pos < (q + 1) * LEN) & (pos - q * LEN < lengths[0:1, q : q + 1])
        valid = valid + ok.astype(F32)
    square = lax.broadcasted_iota(jnp.int32, (tok, tok), 0) == lax.broadcasted_iota(
        jnp.int32, (tok, tok), 1
    )

    def column(row):
        spread = jnp.where(square, jnp.broadcast_to(row, (tok, tok)), 0)
        return jnp.sum(spread.astype(F32), axis=-1, keepdims=True)

    expert_lane = expert_lane.astype(F32)
    first_hot = (column(routes[0, 0:1, :]) == expert_lane).astype(F32)
    second_hot = (column(routes[0, 1:2, :]) == expert_lane).astype(F32)
    chosen = (first_hot + second_hot) * valid
    before = (
        lax.broadcasted_iota(jnp.int32, (tok, tok), 1)
        < lax.broadcasted_iota(jnp.int32, (tok, tok), 0)
    ).astype(BF)
    rank = jnp.dot(before, chosen.astype(BF), preferred_element_type=F32)
    n_main = experts * main
    n_slots = experts * cap
    lanes = -(-n_slots // 128) * 128
    lane = lax.broadcasted_iota(jnp.int32, (1, lanes), 1)
    slot_of = jnp.full((1, lanes), -1, jnp.int32)
    expert_of = jnp.full((1, lanes), -1, jnp.int32)
    for k in range(experts):
        ek = xor(e, k, experts)
        in_main = (lane >= k * main) & (lane < (k + 1) * main)
        low = n_main + k * rest
        in_rest = (lane >= low) & (lane < low + rest)
        slot_of = jnp.where(in_main, lane - k * main, slot_of)
        slot_of = jnp.where(in_rest, lane - low + main, slot_of)
        expert_of = jnp.where(in_main | in_rest, ek, expert_of)
    placing = jnp.zeros((tok, lanes), F32)
    for k in range(experts):
        here = (expert_of == k) & (rank[:, k : k + 1] == slot_of.astype(F32))
        placing = placing + jnp.where(here, chosen[:, k : k + 1], 0.0)
    place_rows = jnp.transpose(placing)[0:n_slots].astype(BF)
    slots = jnp.dot(place_rows, normed, preferred_element_type=F32)

    def place(dc, dx, k):
        turn = 0 if k in turns[0] else 1
        return turn, turn * gc + gc - 1 - dc, dx * span + turns[turn].index(k)

    def rows_a(dc, dx, k):
        _, part, b = place(dc, dx, k)
        return pl.ds(part * chunk + b * main, main)

    def index_b(dc, dx, k):
        return (dc * gx + dx) * experts + k

    x[rows_a(0, 0, 0), :] = slots[0:main].astype(BF)
    x_b[0] = slots[n_main : n_main + rest].astype(BF)
    for k in hop_order:
        out_a[k] = slots[k * main : (k + 1) * main].astype(BF)
        out_b[k] = slots[n_main + k * rest : n_main + (k + 1) * rest].astype(BF)

    waits = []

    def send(src, dst, s_sem, r_sem, target):
        copy = pltpu.make_async_remote_copy(
            src, dst, s_sem, r_sem, device_id=target, device_id_type=MESH
        )
        copy.start()
        waits.append(copy)

    def landed(ref, sem):
        pltpu.make_async_copy(ref, ref, sem).wait()

    half_width = width // 2

    def piece(slot, p):
        if p < 2:
            return x.at[rows_a(*slot), p * half_width : (p + 1) * half_width]
        return x_b.at[index_b(*slot)]

    def arrived(slot, p):
        landed(piece(slot, p), ra.at[3 * index_b(*slot) + p])

    def forward(slot_from, slot_to, p, sems, base, target):
        send(
            piece(slot_from, p), piece(slot_to, p), sems.at[3 * base + p],
            ra.at[3 * index_b(*slot_to) + p], target,
        )

    for k in hop_order:
        target = dev(xor(e, k, experts), xi, ci)
        for p in range(3):
            src = out_a.at[k, :, p * half_width : (p + 1) * half_width] if p < 2 else out_b.at[k]
            send(
                src, piece((0, 0, k), p), sz.at[3 * k + p], ra.at[3 * index_b(0, 0, k) + p], target
            )

    core_dev = dev(e, xi, lax.rem(ci + 1, gc))

    def from_column(k):
        for p in range(3):
            if k:
                arrived((0, 0, k), p)
            for d in range(1, gx):
                forward(
                    (0, 0, k), (0, d, k), p, sx, (d - 1) * experts + k,
                    dev(e, lax.rem(xi + d, gx), ci),
                )
            forward((0, 0, k), (1, 0, k), p, sc, k, core_dev)

    def from_chips(k):
        for p in range(3):
            for d in range(1, gx):
                arrived((0, d, k), p)
                forward((0, d, k), (1, d, k), p, sc, d * experts + k, core_dev)

    order = [0] + hop_order
    for i, k in enumerate(order):
        from_column(k)
        if i:
            from_chips(order[i - 1])
    from_chips(order[-1])
    for k in order:
        for d in range(gx):
            for p in range(3):
                arrived((1, d, k), p)

    blocks = gx * experts
    for dc in range(gc):
        for turn in range(2):
            for dx in range(gx):
                for k in turns[turn]:
                    _, part, b = place(dc, dx, k)
                    stage[b * rest : (b + 1) * rest, :] = x_b[index_b(dc, dx, k)].astype(F32)
            x[part * chunk + chunk_main : (part + 1) * chunk, :] = stage[...].astype(BF)

    units = win.shape[1]
    tile = min(256, units)
    loads[0].wait()

    @pl.loop(0, units // tile)
    def _(i):
        cols = pl.ds(pl.multiple_of(i * tile, tile), tile)
        act[:, cols] = jnp.maximum(
            jnp.dot(x[...], win[:, cols], preferred_element_type=F32), 0.0
        ).astype(BF)

    loads[1].wait()
    tile2 = 256

    def chip_sum(dx, k):
        turn, _, b = place(0, dx, k)
        top = turn * chunk + b * main
        sum_a = y0[top : top + main, :] + rc_a[turn, b * main : (b + 1) * main, :].astype(F32)
        low = turn * chunk + chunk_main + b * rest
        sum_b = y0[low : low + rest, :] + rc_b[turn, b].astype(F32)
        return sum_a, sum_b

    def second(turn):
        @pl.loop(0, width // tile2)
        def _(i):
            cols = pl.ds(pl.multiple_of(i * tile2, tile2), tile2)
            rows = act[turn * gc * chunk : (turn * gc + 1) * chunk, :]
            part = jnp.dot(rows, wout[:, cols], preferred_element_type=F32)
            core_a[turn, :, cols] = part[0:chunk_main].astype(BF)
            for b in range(gx * span):
                low = chunk_main + b * rest
                core_b[turn, b, :, cols] = part[low : low + rest].astype(BF)

        send(core_a.at[turn], rc_a.at[turn], rc_s.at[2 * turn], rc_r.at[2 * turn], core_dev)
        send(core_b.at[turn], rc_b.at[turn], rc_s.at[2 * turn + 1], rc_r.at[2 * turn + 1], core_dev)

        @pl.loop(0, width // tile2)
        def _(i):
            cols = pl.ds(pl.multiple_of(i * tile2, tile2), tile2)
            rows = act[(turn * gc + 1) * chunk : (turn + 1) * gc * chunk, :]
            y0[turn * chunk : (turn + 1) * chunk, cols] = jnp.dot(
                rows, wout[:, cols], preferred_element_type=F32
            )

        landed(rc_a.at[turn], rc_r.at[2 * turn])
        landed(rc_b.at[turn], rc_r.at[2 * turn + 1])
        for k in turns[turn]:
            for d in range(1, gx):
                o = (d - 1) * experts + k
                sum_a, sum_b = chip_sum(d, k)
                xs_a[o] = sum_a.astype(BF)
                xs_b[o] = sum_b.astype(BF)
                target = dev(e, lax.rem(xi + gx - d, gx), ci)
                send(xs_a.at[o], rx_a.at[o], rx_s.at[2 * o], rx_r.at[2 * o], target)
                send(xs_b.at[o], rx_b.at[o], rx_s.at[2 * o + 1], rx_r.at[2 * o + 1], target)

    second(0)
    second(1)
    for k in back_order:
        sum_a, sum_b = chip_sum(0, k)
        for d in range(1, gx):
            o = (d - 1) * experts + k
            landed(rx_a.at[o], rx_r.at[2 * o])
            landed(rx_b.at[o], rx_r.at[2 * o + 1])
            sum_a = sum_a + rx_a[o].astype(F32)
            sum_b = sum_b + rx_b[o].astype(F32)
        if k:
            zs_a[k] = sum_a.astype(BF)
            zs_b[k] = sum_b.astype(BF)
            target = dev(xor(e, k, experts), xi, ci)
            send(zs_a.at[k], z_a.at[k], rz_s.at[2 * k], rz_r.at[2 * k], target)
            send(zs_b.at[k], z_b.at[k], rz_s.at[2 * k + 1], rz_r.at[2 * k + 1], target)
        else:
            z_all[0:main, :] = sum_a.astype(BF)
            z_stage[0:rest, :] = sum_b

    early[3].wait()
    probs = lax.dot_general(
        normed, router[0], (((1,), (1,)), ((), ())), preferred_element_type=F32
    )
    probs = jnp.exp(probs - jnp.max(probs, axis=-1, keepdims=True))
    probs = probs / jnp.sum(probs, axis=-1, keepdims=True)
    prob_first = jnp.sum(probs * first_hot, axis=-1, keepdims=True)
    prob_second = jnp.sum(probs * second_hot, axis=-1, keepdims=True)
    gate = (prob_first * first_hot + prob_second * second_hot) / (prob_first + prob_second)
    combine = jnp.zeros((tok, lanes), F32)
    for k in range(experts):
        combine = combine + jnp.where(expert_of == k, gate[:, k : k + 1], 0.0)
    combine = (combine * placing)[:, 0:n_slots]
    high = combine.astype(BF)
    low = (combine - high.astype(F32)).astype(BF)

    early[4].wait()
    learner_in = student[0]
    shifted = learner_in - jnp.max(learner_in, axis=-1, keepdims=True)
    learner = shifted - jnp.log(jnp.sum(jnp.exp(shifted), axis=-1, keepdims=True))
    target_col = column(targets[0:1, :])
    vocab = student.shape[2]
    picked = lax.broadcasted_iota(jnp.int32, (tok, vocab), 1).astype(F32) == target_col
    hit = jnp.sum(jnp.where(picked, learner, 0.0), axis=-1, keepdims=True)
    loads[2].wait()

    for k in hop_order:
        landed(z_a.at[k], rz_r.at[2 * k])
        landed(z_b.at[k], rz_r.at[2 * k + 1])
        z_all[k * main : (k + 1) * main, :] = z_a[k]
        z_stage[k * rest : (k + 1) * rest, :] = z_b[k].astype(F32)
    z_all[n_main:, :] = z_stage[...].astype(BF)
    back = z_all[...]
    moe = jnp.dot(high, back, preferred_element_type=F32) + jnp.dot(
        low, back, preferred_element_type=F32
    )
    out = (mid[...] + moe).astype(BF)
    out_stage[...] = out
    out_copy = pltpu.make_async_copy(out_stage, layer_out.at[0], wsem.at[8])
    out_copy.start()

    final = layer_norm(out.astype(F32), gains[2]).astype(BF)
    logits = jnp.dot(final, short[...], preferred_element_type=F32)
    logits = logits - jnp.max(logits, axis=-1, keepdims=True)
    teacher = logits - jnp.log(jnp.sum(jnp.exp(logits), axis=-1, keepdims=True))
    token_loss = jnp.sum(jnp.exp(teacher) * (teacher - learner), axis=-1, keepdims=True) - hit
    counted = jnp.where(is_decoder, valid, 0.0)
    loss_sum = jnp.sum(token_loss * counted, axis=0, keepdims=True)
    loss_count = jnp.sum(counted, axis=0, keepdims=True)
    spot = lax.broadcasted_iota(jnp.int32, lsend.shape, 1)
    pair = jnp.where(spot == 0, loss_sum, jnp.where(spot == 1, loss_count, 0.0))
    lsend[...] = pair

    @pl.when(is_decoder)
    def _():
        mine = (seg - half_seg) * n_exp
        lrecv[mine + me] = pair
        for ds in range(n_seg):
            for d in range(n_exp):
                if ds or d:
                    pltpu.make_async_remote_copy(
                        lsend, lrecv.at[mine + me], l_s.at[ds * n_exp + d], l_r.at[mine + d],
                        device_id=peer(ds, d), device_id_type=MESH,
                    ).start()

    for q in range(n_seg - half_seg):
        for d in range(n_exp):
            source = q * n_exp + lax.rem(me + n_exp - d, n_exp)
            if d:
                landed(lrecv.at[source], l_r.at[q * n_exp + d])
            else:
                @pl.when(seg != q + half_seg)
                def _():
                    landed(lrecv.at[source], l_r.at[q * n_exp])

    total = lrecv[0]
    for i in range(1, (n_seg - half_seg) * n_exp):
        total = total + lrecv[i]
    loss_out[...] = total[0:1, 0:1] / total[0:1, 1:2]

    @pl.when(is_decoder)
    def _():
        for i in range(1, n_seg * n_exp):
            pltpu.make_async_copy(lsend, lsend, l_s.at[i]).wait()

    out_copy.wait()
    for copy in waits:
        copy.wait_send()

    @pl.when(seg < half_seg)
    def _():
        len_copy.wait_send()
        for copy in mem_copies:
            copy.wait_send()


def local(
    hidden, memory, lengths, memory_lengths, routes, norm_gain, router,
    w_in, w_out, shortlist, student, targets,
):
    n_seg = lax.axis_size("segment")
    n_exp = lax.axis_size("expert")
    experts = router.shape[2]
    group = n_exp // experts
    gc = 2
    gx = group // gc
    tok, width = hidden.shape[1], hidden.shape[2]
    units = w_in.shape[2]
    vocab = shortlist.shape[2]
    cap = 5 * tok // 8
    main = cap // 16 * 16
    rest = cap - main
    blocks = gx * experts
    half_rows = blocks * cap
    span = experts // 2
    vm = pl.BlockSpec(memory_space=pltpu.VMEM)
    hbm = pl.BlockSpec(memory_space=pl.ANY)
    v = pltpu.VMEM
    dma = pltpu.SemaphoreType.DMA
    nx = max(gx - 1, 1) * experts
    scratch = [
        v((1, tok, width), BF), v((1, 2, tok), jnp.int32), v((3, 1, width), F32),
        v((1, experts, width), BF), v((1, tok, vocab), F32), v((tok, width), BF),
        v((width, units), BF), v((units, width), BF), v((width, vocab), BF),
        v((tok, width), BF), v((8, 128), jnp.int32), v((8, 128), jnp.int32), v((tok, width), F32),
        v((experts, main, width), BF), v((experts, rest, width), BF),
        v((gc * half_rows, width), BF), v((gc * blocks, rest, width), BF),
        v((gx * span * rest, width), F32), v((gc * half_rows, units), BF), v((half_rows, width), F32),
        v((2, gx * span * main, width), BF), v((2, gx * span, rest, width), BF),
        v((2, gx * span * main, width), BF), v((2, gx * span, rest, width), BF),
        v((nx, main, width), BF), v((nx, rest, width), BF),
        v((nx, main, width), BF), v((nx, rest, width), BF),
        v((experts, main, width), BF), v((experts, rest, width), BF),
        v((experts, main, width), BF), v((experts, rest, width), BF),
        v((experts * cap, width), BF), v((experts * rest, width), F32),
        v((1, 128), F32), v(((n_seg - n_seg // 2) * n_exp, 1, 128), F32),
        dma((9,)), dma((10,)), dma((3 * gc * blocks,)),
        dma((3 * experts,)), dma((3 * nx,)), dma((3 * blocks,)),
        dma((4,)), dma((4,)), dma((2 * nx,)), dma((2 * nx,)),
        dma((2 * experts,)), dma((2 * experts,)),
        dma((n_seg * n_exp,)), dma(((n_seg - n_seg // 2) * n_exp,)),
    ]
    layer_out, loss = pl.pallas_call(
        functools.partial(kernel, n_seg, n_exp, experts, gx, gc),
        out_shape=(
            jax.ShapeDtypeStruct((1, tok, width), BF),
            jax.ShapeDtypeStruct((1, 1), F32),
        ),
        in_specs=[hbm, hbm, vm, vm, hbm, hbm, hbm, hbm, hbm, hbm, hbm, vm],
        out_specs=(hbm, vm),
        scratch_shapes=scratch,
        compiler_params=pltpu.CompilerParams(
            collective_id=0, has_side_effects=True, vmem_limit_bytes=60 * 1024 * 1024
        ),
    )(
        hidden, memory, lengths, memory_lengths, jnp.swapaxes(routes, 1, 2),
        jnp.swapaxes(norm_gain, 0, 1), jnp.swapaxes(router, 1, 2),
        w_in, w_out, shortlist, student, targets,
    )
    return layer_out, loss[0, 0]


def solution(mesh):
    placed = (
        P("segment", "expert", None),
        P("segment", "expert", None),
        P("segment", "expert"),
        P("segment", "expert"),
        P("segment", "expert", None),
        P("segment", None, None),
        P("segment", None, None),
        P("segment", None, "expert"),
        P("segment", "expert", None),
        P("segment", None, None),
        P("segment", "expert", None),
        P("segment", "expert"),
    )
    return jax.shard_map(
        local,
        mesh=mesh,
        in_specs=placed,
        out_specs=(P("segment", "expert", None), P()),
        check_vma=False,
    )
```

```python
import functools
import math

import jax
import jax.numpy as jnp
from jax import lax
from jax.experimental import pallas as pl
from jax.experimental.pallas import tpu as pltpu
from jax.sharding import PartitionSpec as P

HEAD_DIM = 128
LEN = 32
EPS = 1e-05
MESH = pl.DeviceIdType.MESH
BF = jnp.bfloat16
F32 = jnp.float32


def layer_norm(values, gain_row):
    centred = values - jnp.mean(values, axis=-1, keepdims=True)
    spread = jnp.mean(centred * centred, axis=-1, keepdims=True)
    return centred * lax.rsqrt(spread + EPS) * gain_row


def xor(a, k, count):
    out = 0
    bit = 1
    while bit < count:
        out = out + lax.rem(a // bit + (k // bit) % 2, 2) * bit
        bit *= 2
    return out


def kernel(
    n_seg, n_exp, experts, gx, gc,
    hidden_any, memory, lengths, memory_lengths, routes_any, gain_any, router_any,
    w_in, w_out, shortlist, student_any, targets,
    layer_out, loss_out,
    hidden, routes, norm_gain, router, student, out_stage,
    win, wout, short, kmem, klen_src, klen, mid,
    out_a, out_b, x, x_b, stage, act, y0,
    core_a, core_b, rc_a, rc_b, xs_a, xs_b, rx_a, rx_b, zs_a, zs_b, z_a, z_b, z_all, z_stage,
    lsend, l_plane, l_hop, l_seg,
    wsem, msem, ra, sz, sx, sc, rc_s, rc_r, rx_s, rx_r, rz_s, rz_r, l_s, l_r,
):
    seg = lax.axis_index("segment")
    me = lax.axis_index("expert")
    half_seg = n_seg // 2
    group = gx * gc
    e = me // group
    j = lax.rem(me, group)
    xi = j // gc
    ci = lax.rem(j, gc)
    tok = hidden.shape[1]
    width = hidden.shape[2]
    heads = width // HEAD_DIM
    cap = 5 * tok // 8
    main = cap // 16 * 16
    rest = cap - main
    hop_order = list(range(experts - 1, 0, -1))
    back_order = hop_order + [0]
    span = experts
    turns = [back_order]
    chunk_main = gx * span * main
    chunk = gx * span * cap

    def dev(e2, x2, c2):
        return (seg, (e2 * gx + x2) * gc + c2)

    barrier = pltpu.get_barrier_semaphore()
    def plane_peer(d):
        return (seg, e * group + lax.rem(j + d, group))

    def hop_peer(k):
        return (seg, xor(e, k, experts) * group + j)

    def seg_peer(d):
        return (lax.rem(seg + d, n_seg), me)

    partners = [plane_peer(d) for d in range(1, group)]
    partners += [hop_peer(k) for k in range(1, experts)]
    partners += [seg_peer(d) for d in range(1, n_seg)]
    for target in partners:
        pl.semaphore_signal(barrier, inc=1, device_id=target, device_id_type=MESH)

    early = [
        pltpu.make_async_copy(hidden_any, hidden, wsem.at[3]),
        pltpu.make_async_copy(gain_any, norm_gain, wsem.at[4]),
        pltpu.make_async_copy(routes_any, routes, wsem.at[5]),
        pltpu.make_async_copy(router_any, router, wsem.at[6]),
        pltpu.make_async_copy(student_any, student, wsem.at[7]),
    ]
    for load in early:
        load.start()
    loads = [
        pltpu.make_async_copy(w_in.at[0], win, wsem.at[0]),
        pltpu.make_async_copy(w_out.at[0], wout, wsem.at[1]),
        pltpu.make_async_copy(shortlist.at[0], short, wsem.at[2]),
    ]
    for load in loads:
        load.start()

    klen_src[...] = jnp.broadcast_to(memory_lengths[0:1, 0:1], klen_src.shape)
    for q in range(1, tok // LEN):
        klen_src[q : q + 1, :] = jnp.broadcast_to(memory_lengths[0:1, q : q + 1], (1, 128))
    early[0].wait()
    early[1].wait()
    gains = [norm_gain[i] for i in range(3)]
    states = hidden[0].astype(F32)
    pl.semaphore_wait(barrier, len(partners))

    is_decoder = seg >= half_seg
    to_seg = lax.rem(seg + half_seg, n_seg)
    mem_parts = 4 if heads % 4 == 0 else 1
    mem_width = width // mem_parts
    mem_copies = []
    for p in range(mem_parts):
        part = slice(p * mem_width, (p + 1) * mem_width)
        mem_copies.append(
            pltpu.make_async_remote_copy(
                memory.at[0, :, part], kmem.at[:, part], msem.at[2 + p], msem.at[6 + p],
                device_id=(to_seg, me), device_id_type=MESH,
            )
        )
    len_copy = pltpu.make_async_remote_copy(
        klen_src, klen, msem.at[0], msem.at[1], device_id=(to_seg, me), device_id_type=MESH
    )

    @pl.when(seg < half_seg)
    def _():
        len_copy.start()
        for copy in mem_copies:
            copy.start()
        mid[...] = states

    @pl.when(seg >= half_seg)
    def _():
        queries = layer_norm(states, gains[0]).astype(BF)
        len_copy.wait_recv()
        col = lax.broadcasted_iota(jnp.int32, (tok, tok), 1)
        row = lax.broadcasted_iota(jnp.int32, (tok, tok), 0)
        klen_v = klen[...]
        allowed = jnp.zeros((tok, tok), jnp.bool_)
        for q in range(tok // LEN):
            inside = (col >= q * LEN) & (col - q * LEN < klen_v[q : q + 1, 0:1])
            inside = inside & (col < (q + 1) * LEN) & (row >= q * LEN) & (row < (q + 1) * LEN)
            allowed = allowed | inside
        for p in range(mem_parts):
            mem_copies[p].wait_recv()
            span_heads = range(p * heads // mem_parts, (p + 1) * heads // mem_parts)
            parts = [slice(h * HEAD_DIM, (h + 1) * HEAD_DIM) for h in span_heads]
            scores = jnp.concatenate(
                [
                    jnp.where(
                        allowed,
                        lax.dot_general(
                            queries[:, part], kmem[:, part], (((1,), (1,)), ((), ())),
                            preferred_element_type=F32,
                        )
                        * (1.0 / math.sqrt(HEAD_DIM)),
                        -1e30,
                    )
                    for part in parts
                ],
                axis=0,
            )
            top = jnp.max(scores, axis=-1, keepdims=True)
            raised = jnp.exp(scores - top)
            weights = (raised / jnp.sum(raised, axis=-1, keepdims=True)).astype(BF)
            for i, part in enumerate(parts):
                mid[:, part] = states[:, part] + jnp.dot(
                    weights[i * tok : (i + 1) * tok], kmem[:, part], preferred_element_type=F32
                )

    normed = layer_norm(mid[...], gains[1]).astype(BF)

    early[2].wait()
    expert_lane = lax.broadcasted_iota(jnp.int32, (tok, experts), 1)
    pos = lax.broadcasted_iota(jnp.int32, (tok, 1), 0)
    valid = jnp.zeros((tok, 1), F32)
    for q in range(tok // LEN):
        ok = (pos >= q * LEN) & (pos < (q + 1) * LEN) & (pos - q * LEN < lengths[0:1, q : q + 1])
        valid = valid + ok.astype(F32)
    square = lax.broadcasted_iota(jnp.int32, (tok, tok), 0) == lax.broadcasted_iota(
        jnp.int32, (tok, tok), 1
    )

    def column(row):
        spread = jnp.where(square, jnp.broadcast_to(row, (tok, tok)), 0)
        return jnp.sum(spread.astype(F32), axis=-1, keepdims=True)

    expert_lane = expert_lane.astype(F32)
    first_hot = (column(routes[0, 0:1, :]) == expert_lane).astype(F32)
    second_hot = (column(routes[0, 1:2, :]) == expert_lane).astype(F32)
    chosen = (first_hot + second_hot) * valid
    before = (
        lax.broadcasted_iota(jnp.int32, (tok, tok), 1)
        < lax.broadcasted_iota(jnp.int32, (tok, tok), 0)
    ).astype(BF)
    rank = jnp.dot(before, chosen.astype(BF), preferred_element_type=F32)
    n_main = experts * main
    n_slots = experts * cap
    lanes = -(-n_slots // 128) * 128
    lane = lax.broadcasted_iota(jnp.int32, (1, lanes), 1)
    slot_of = jnp.full((1, lanes), -1, jnp.int32)
    expert_of = jnp.full((1, lanes), -1, jnp.int32)
    for k in range(experts):
        ek = xor(e, k, experts)
        in_main = (lane >= k * main) & (lane < (k + 1) * main)
        low = n_main + k * rest
        in_rest = (lane >= low) & (lane < low + rest)
        slot_of = jnp.where(in_main, lane - k * main, slot_of)
        slot_of = jnp.where(in_rest, lane - low + main, slot_of)
        expert_of = jnp.where(in_main | in_rest, ek, expert_of)
    placing = jnp.zeros((tok, lanes), F32)
    for k in range(experts):
        here = (expert_of == k) & (rank[:, k : k + 1] == slot_of.astype(F32))
        placing = placing + jnp.where(here, chosen[:, k : k + 1], 0.0)
    place_rows = jnp.transpose(placing)[0:n_slots].astype(BF)
    slots = jnp.dot(place_rows, normed, preferred_element_type=F32)

    def place(dc, dx, k):
        turn = 0 if k in turns[0] else 1
        return turn, turn * gc + gc - 1 - dc, dx * span + turns[turn].index(k)

    def rows_a(dc, dx, k):
        _, part, b = place(dc, dx, k)
        return pl.ds(part * chunk + b * main, main)

    def index_b(dc, dx, k):
        return (dc * gx + dx) * experts + k

    x[rows_a(0, 0, 0), :] = slots[0:main].astype(BF)
    x_b[0] = slots[n_main : n_main + rest].astype(BF)
    for k in hop_order:
        out_a[k] = slots[k * main : (k + 1) * main].astype(BF)
        out_b[k] = slots[n_main + k * rest : n_main + (k + 1) * rest].astype(BF)

    waits = []

    def send(src, dst, s_sem, r_sem, target):
        copy = pltpu.make_async_remote_copy(
            src, dst, s_sem, r_sem, device_id=target, device_id_type=MESH
        )
        copy.start()
        waits.append(copy)

    def landed(ref, sem):
        pltpu.make_async_copy(ref, ref, sem).wait()

    half_width = width // 2

    def piece(slot, p):
        if p < 2:
            return x.at[rows_a(*slot), p * half_width : (p + 1) * half_width]
        return x_b.at[index_b(*slot)]

    def arrived(slot, p):
        landed(piece(slot, p), ra.at[3 * index_b(*slot) + p])

    def forward(slot_from, slot_to, p, sems, base, target):
        send(
            piece(slot_from, p), piece(slot_to, p), sems.at[3 * base + p],
            ra.at[3 * index_b(*slot_to) + p], target,
        )

    for k in hop_order:
        target = dev(xor(e, k, experts), xi, ci)
        for p in range(3):
            src = out_a.at[k, :, p * half_width : (p + 1) * half_width] if p < 2 else out_b.at[k]
            send(
                src, piece((0, 0, k), p), sz.at[3 * k + p], ra.at[3 * index_b(0, 0, k) + p], target
            )

    core_dev = dev(e, xi, lax.rem(ci + 1, gc))

    def from_column(k):
        for p in range(3):
            if k:
                arrived((0, 0, k), p)
            for d in range(1, gx):
                forward(
                    (0, 0, k), (0, d, k), p, sx, (d - 1) * experts + k,
                    dev(e, lax.rem(xi + d, gx), ci),
                )
            forward((0, 0, k), (1, 0, k), p, sc, k, core_dev)

    def from_chips(k):
        for p in range(3):
            for d in range(1, gx):
                arrived((0, d, k), p)
                forward((0, d, k), (1, d, k), p, sc, d * experts + k, core_dev)

    order = [0] + hop_order
    for i, k in enumerate(order):
        from_column(k)
        if i:
            from_chips(order[i - 1])
    from_chips(order[-1])
    for k in order:
        for d in range(gx):
            for p in range(3):
                arrived((1, d, k), p)

    blocks = gx * experts
    for dc in range(gc):
        for turn in range(len(turns)):
            for dx in range(gx):
                for k in turns[turn]:
                    _, part, b = place(dc, dx, k)
                    stage[b * rest : (b + 1) * rest, :] = x_b[index_b(dc, dx, k)].astype(F32)
            x[part * chunk + chunk_main : (part + 1) * chunk, :] = stage[...].astype(BF)

    units = win.shape[1]
    tile = min(256, units)
    loads[0].wait()

    @pl.loop(0, units // tile)
    def _(i):
        cols = pl.ds(pl.multiple_of(i * tile, tile), tile)
        act[:, cols] = jnp.maximum(
            jnp.dot(x[...], win[:, cols], preferred_element_type=F32), 0.0
        ).astype(BF)

    loads[1].wait()
    tile2 = 256

    def chip_sum(dx, k):
        turn, _, b = place(0, dx, k)
        top = turn * chunk + b * main
        sum_a = y0[top : top + main, :] + rc_a[turn, b * main : (b + 1) * main, :].astype(F32)
        low = turn * chunk + chunk_main + b * rest
        sum_b = y0[low : low + rest, :] + rc_b[turn, b].astype(F32)
        return sum_a, sum_b

    def second(turn):
        @pl.loop(0, width // tile2)
        def _(i):
            cols = pl.ds(pl.multiple_of(i * tile2, tile2), tile2)
            rows = act[turn * gc * chunk : (turn * gc + 1) * chunk, :]
            part = jnp.dot(rows, wout[:, cols], preferred_element_type=F32)
            core_a[turn, :, cols] = part[0:chunk_main].astype(BF)
            for b in range(gx * span):
                low = chunk_main + b * rest
                core_b[turn, b, :, cols] = part[low : low + rest].astype(BF)

        send(core_a.at[turn], rc_a.at[turn], rc_s.at[2 * turn], rc_r.at[2 * turn], core_dev)
        send(core_b.at[turn], rc_b.at[turn], rc_s.at[2 * turn + 1], rc_r.at[2 * turn + 1], core_dev)

        @pl.loop(0, width // tile2)
        def _(i):
            cols = pl.ds(pl.multiple_of(i * tile2, tile2), tile2)
            rows = act[(turn * gc + 1) * chunk : (turn + 1) * gc * chunk, :]
            y0[turn * chunk : (turn + 1) * chunk, cols] = jnp.dot(
                rows, wout[:, cols], preferred_element_type=F32
            )

        landed(rc_a.at[turn], rc_r.at[2 * turn])
        landed(rc_b.at[turn], rc_r.at[2 * turn + 1])
        for k in turns[turn]:
            for d in range(1, gx):
                o = (d - 1) * experts + k
                sum_a, sum_b = chip_sum(d, k)
                xs_a[o] = sum_a.astype(BF)
                xs_b[o] = sum_b.astype(BF)
                target = dev(e, lax.rem(xi + gx - d, gx), ci)
                send(xs_a.at[o], rx_a.at[o], rx_s.at[2 * o], rx_r.at[2 * o], target)
                send(xs_b.at[o], rx_b.at[o], rx_s.at[2 * o + 1], rx_r.at[2 * o + 1], target)

    second(0)
    for k in back_order:
        sum_a, sum_b = chip_sum(0, k)
        for d in range(1, gx):
            o = (d - 1) * experts + k
            landed(rx_a.at[o], rx_r.at[2 * o])
            landed(rx_b.at[o], rx_r.at[2 * o + 1])
            sum_a = sum_a + rx_a[o].astype(F32)
            sum_b = sum_b + rx_b[o].astype(F32)
        if k:
            zs_a[k] = sum_a.astype(BF)
            zs_b[k] = sum_b.astype(BF)
            target = dev(xor(e, k, experts), xi, ci)
            send(zs_a.at[k], z_a.at[k], rz_s.at[2 * k], rz_r.at[2 * k], target)
            send(zs_b.at[k], z_b.at[k], rz_s.at[2 * k + 1], rz_r.at[2 * k + 1], target)
        else:
            z_all[0:main, :] = sum_a.astype(BF)
            z_stage[0:rest, :] = sum_b

    early[3].wait()
    probs = lax.dot_general(
        normed, router[0], (((1,), (1,)), ((), ())), preferred_element_type=F32
    )
    probs = jnp.exp(probs - jnp.max(probs, axis=-1, keepdims=True))
    probs = probs / jnp.sum(probs, axis=-1, keepdims=True)
    prob_first = jnp.sum(probs * first_hot, axis=-1, keepdims=True)
    prob_second = jnp.sum(probs * second_hot, axis=-1, keepdims=True)
    gate = (prob_first * first_hot + prob_second * second_hot) / (prob_first + prob_second)
    combine = jnp.zeros((tok, lanes), F32)
    for k in range(experts):
        combine = combine + jnp.where(expert_of == k, gate[:, k : k + 1], 0.0)
    combine = (combine * placing)[:, 0:n_slots]
    high = combine.astype(BF)
    low = (combine - high.astype(F32)).astype(BF)

    early[4].wait()
    learner_in = student[0]
    shifted = learner_in - jnp.max(learner_in, axis=-1, keepdims=True)
    learner = shifted - jnp.log(jnp.sum(jnp.exp(shifted), axis=-1, keepdims=True))
    target_col = column(targets[0:1, :])
    vocab = student.shape[2]
    picked = lax.broadcasted_iota(jnp.int32, (tok, vocab), 1).astype(F32) == target_col
    hit = jnp.sum(jnp.where(picked, learner, 0.0), axis=-1, keepdims=True)
    loads[2].wait()

    for k in hop_order:
        landed(z_a.at[k], rz_r.at[2 * k])
        landed(z_b.at[k], rz_r.at[2 * k + 1])
        z_all[k * main : (k + 1) * main, :] = z_a[k]
        z_stage[k * rest : (k + 1) * rest, :] = z_b[k].astype(F32)
    z_all[n_main:, :] = z_stage[...].astype(BF)
    back = z_all[...]
    moe = jnp.dot(high, back, preferred_element_type=F32) + jnp.dot(
        low, back, preferred_element_type=F32
    )
    out = (mid[...] + moe).astype(BF)
    out_stage[...] = out
    out_copy = pltpu.make_async_copy(out_stage, layer_out.at[0], wsem.at[8])
    out_copy.start()

    final = layer_norm(out.astype(F32), gains[2]).astype(BF)
    logits = jnp.dot(final, short[...], preferred_element_type=F32)
    logits = logits - jnp.max(logits, axis=-1, keepdims=True)
    teacher = logits - jnp.log(jnp.sum(jnp.exp(logits), axis=-1, keepdims=True))
    token_loss = jnp.sum(jnp.exp(teacher) * (teacher - learner), axis=-1, keepdims=True) - hit
    counted = jnp.where(is_decoder, valid, 0.0)
    loss_sum = jnp.sum(token_loss * counted, axis=0, keepdims=True)
    loss_count = jnp.sum(counted, axis=0, keepdims=True)
    spot = lax.broadcasted_iota(jnp.int32, (1, 128), 1)
    pair = jnp.where(spot == 0, loss_sum, jnp.where(spot == 1, loss_count, 0.0))

    def added(value, out_row, table, here, count, peers, arrivals, base):
        out_row[...] = value
        table[here] = value
        for i, target in enumerate(peers):
            send(out_row, table.at[here], l_s.at[base + i], l_r.at[base + i], target)
        for i, source in enumerate(arrivals):
            landed(table.at[source], l_r.at[base + i])
        result = table[0]
        for i in range(1, count):
            result = result + table[i]
        return result

    total = added(
        pair, lsend.at[0], l_plane, j, group, partners[0 : group - 1],
        [lax.rem(j + group - d, group) for d in range(1, group)], 0,
    )
    total = added(
        total, lsend.at[1], l_hop, e, experts, partners[group - 1 : group + experts - 2],
        [xor(e, k, experts) for k in range(1, experts)], group - 1,
    )
    total = added(
        total, lsend.at[2], l_seg, seg, n_seg, partners[group + experts - 2 :],
        [lax.rem(seg + n_seg - d, n_seg) for d in range(1, n_seg)], group + experts - 2,
    )
    loss_out[...] = total[0:1, 0:1] / total[0:1, 1:2]
    out_copy.wait()
    for copy in waits:
        copy.wait_send()

    @pl.when(seg < half_seg)
    def _():
        len_copy.wait_send()
        for copy in mem_copies:
            copy.wait_send()


def local(
    hidden, memory, lengths, memory_lengths, routes, norm_gain, router,
    w_in, w_out, shortlist, student, targets,
):
    n_seg = lax.axis_size("segment")
    n_exp = lax.axis_size("expert")
    experts = router.shape[2]
    group = n_exp // experts
    gc = 2
    gx = group // gc
    tok, width = hidden.shape[1], hidden.shape[2]
    units = w_in.shape[2]
    vocab = shortlist.shape[2]
    cap = 5 * tok // 8
    main = cap // 16 * 16
    rest = cap - main
    blocks = gx * experts
    half_rows = blocks * cap
    span = experts
    vm = pl.BlockSpec(memory_space=pltpu.VMEM)
    hbm = pl.BlockSpec(memory_space=pl.ANY)
    v = pltpu.VMEM
    dma = pltpu.SemaphoreType.DMA
    nx = max(gx - 1, 1) * experts
    scratch = [
        v((1, tok, width), BF), v((1, 2, tok), jnp.int32), v((3, 1, width), F32),
        v((1, experts, width), BF), v((1, tok, vocab), F32), v((tok, width), BF),
        v((width, units), BF), v((units, width), BF), v((width, vocab), BF),
        v((tok, width), BF), v((8, 128), jnp.int32), v((8, 128), jnp.int32), v((tok, width), F32),
        v((experts, main, width), BF), v((experts, rest, width), BF),
        v((gc * half_rows, width), BF), v((gc * blocks, rest, width), BF),
        v((gx * span * rest, width), F32), v((gc * half_rows, units), BF), v((half_rows, width), F32),
        v((1, gx * span * main, width), BF), v((1, gx * span, rest, width), BF),
        v((1, gx * span * main, width), BF), v((1, gx * span, rest, width), BF),
        v((nx, main, width), BF), v((nx, rest, width), BF),
        v((nx, main, width), BF), v((nx, rest, width), BF),
        v((experts, main, width), BF), v((experts, rest, width), BF),
        v((experts, main, width), BF), v((experts, rest, width), BF),
        v((experts * cap, width), BF), v((experts * rest, width), F32),
        v((3, 1, 128), F32), v((group, 1, 128), F32), v((experts, 1, 128), F32), v((n_seg, 1, 128), F32),
        dma((9,)), dma((10,)), dma((3 * gc * blocks,)),
        dma((3 * experts,)), dma((3 * nx,)), dma((3 * blocks,)),
        dma((4,)), dma((4,)), dma((2 * nx,)), dma((2 * nx,)),
        dma((2 * experts,)), dma((2 * experts,)),
        dma((group + experts + n_seg,)), dma((group + experts + n_seg,)),
    ]
    layer_out, loss = pl.pallas_call(
        functools.partial(kernel, n_seg, n_exp, experts, gx, gc),
        out_shape=(
            jax.ShapeDtypeStruct((1, tok, width), BF),
            jax.ShapeDtypeStruct((1, 1), F32),
        ),
        in_specs=[hbm, hbm, vm, vm, hbm, hbm, hbm, hbm, hbm, hbm, hbm, vm],
        out_specs=(hbm, vm),
        scratch_shapes=scratch,
        compiler_params=pltpu.CompilerParams(
            collective_id=0, has_side_effects=True, vmem_limit_bytes=60 * 1024 * 1024
        ),
    )(
        hidden, memory, lengths, memory_lengths, jnp.swapaxes(routes, 1, 2),
        jnp.swapaxes(norm_gain, 0, 1), jnp.swapaxes(router, 1, 2),
        w_in, w_out, shortlist, student, targets,
    )
    return layer_out, loss[0, 0]


def solution(mesh):
    placed = (
        P("segment", "expert", None),
        P("segment", "expert", None),
        P("segment", "expert"),
        P("segment", "expert"),
        P("segment", "expert", None),
        P("segment", None, None),
        P("segment", None, None),
        P("segment", None, "expert"),
        P("segment", "expert", None),
        P("segment", None, None),
        P("segment", "expert", None),
        P("segment", "expert"),
    )
    return jax.shard_map(
        local,
        mesh=mesh,
        in_specs=placed,
        out_specs=(P("segment", "expert", None), P()),
        check_vma=False,
    )
```

```python
import functools
import math

import jax
import jax.numpy as jnp
from jax import lax
from jax.experimental import pallas as pl
from jax.experimental.pallas import tpu as pltpu
from jax.sharding import PartitionSpec as P

HEAD_DIM = 128
LEN = 32
EPS = 1e-05
MESH = pl.DeviceIdType.MESH
BF = jnp.bfloat16
F32 = jnp.float32


def layer_norm(values, gain_row):
    centred = values - jnp.mean(values, axis=-1, keepdims=True)
    spread = jnp.mean(centred * centred, axis=-1, keepdims=True)
    return centred * lax.rsqrt(spread + EPS) * gain_row


def xor(a, k, count):
    out = 0
    bit = 1
    while bit < count:
        out = out + lax.rem(a // bit + (k // bit) % 2, 2) * bit
        bit *= 2
    return out


def kernel(
    n_seg, n_exp, experts, gx, gc,
    hidden_any, memory, lengths, memory_lengths, routes_any, gain_any, router_any,
    w_in, w_out, shortlist, student_any, targets,
    layer_out, loss_out,
    hidden, routes, norm_gain, router, student, out_stage,
    win, wout, short, kmem, klen_src, klen, mid,
    out_a, out_b, x, x_b, stage, act, y0,
    core_a, core_b, rc_a, rc_b, xs_a, xs_b, rx_a, rx_b, zs_a, zs_b, z_a, z_b, z_all, z_stage,
    lsend, lrecv,
    wsem, msem, ra, sz, sx, sc, rc_s, rc_r, rx_s, rx_r, rz_s, rz_r, l_s, l_r,
):
    seg = lax.axis_index("segment")
    me = lax.axis_index("expert")
    half_seg = n_seg // 2
    group = gx * gc
    e = me // group
    j = lax.rem(me, group)
    xi = j // gc
    ci = lax.rem(j, gc)
    tok = hidden.shape[1]
    width = hidden.shape[2]
    heads = width // HEAD_DIM
    cap = 5 * tok // 8
    main = cap // 16 * 16
    rest = cap - main
    hop_order = list(range(experts - 1, 0, -1))
    back_order = hop_order + [0]
    span = experts
    turns = [back_order]
    chunk_main = gx * span * main
    chunk = gx * span * cap

    def peer(ds, d):
        return (lax.rem(seg + ds, n_seg), lax.rem(me + d, n_exp))

    def dev(e2, x2, c2):
        return (seg, (e2 * gx + x2) * gc + c2)

    barrier = pltpu.get_barrier_semaphore()
    for ds in range(n_seg):
        for d in range(n_exp):
            if ds or d:
                pl.semaphore_signal(
                    barrier, inc=1, device_id=peer(ds, d), device_id_type=MESH
                )

    early = [
        pltpu.make_async_copy(hidden_any, hidden, wsem.at[3]),
        pltpu.make_async_copy(gain_any, norm_gain, wsem.at[4]),
        pltpu.make_async_copy(routes_any, routes, wsem.at[5]),
        pltpu.make_async_copy(router_any, router, wsem.at[6]),
        pltpu.make_async_copy(student_any, student, wsem.at[7]),
    ]
    for load in early:
        load.start()
    loads = [
        pltpu.make_async_copy(w_in.at[0], win, wsem.at[0]),
        pltpu.make_async_copy(w_out.at[0], wout, wsem.at[1]),
        pltpu.make_async_copy(shortlist.at[0], short, wsem.at[2]),
    ]
    for load in loads:
        load.start()

    klen_src[...] = jnp.broadcast_to(memory_lengths[0:1, 0:1], klen_src.shape)
    for q in range(1, tok // LEN):
        klen_src[q : q + 1, :] = jnp.broadcast_to(memory_lengths[0:1, q : q + 1], (1, 128))
    early[0].wait()
    early[1].wait()
    gains = [norm_gain[i] for i in range(3)]
    states = hidden[0].astype(F32)
    pl.semaphore_wait(barrier, n_exp * n_seg - 1)

    is_decoder = seg >= half_seg
    to_seg = lax.rem(seg + half_seg, n_seg)
    mem_parts = 4 if heads % 4 == 0 else 1
    mem_width = width // mem_parts
    mem_copies = []
    for p in range(mem_parts):
        part = slice(p * mem_width, (p + 1) * mem_width)
        mem_copies.append(
            pltpu.make_async_remote_copy(
                memory.at[0, :, part], kmem.at[:, part], msem.at[2 + p], msem.at[6 + p],
                device_id=(to_seg, me), device_id_type=MESH,
            )
        )
    len_copy = pltpu.make_async_remote_copy(
        klen_src, klen, msem.at[0], msem.at[1], device_id=(to_seg, me), device_id_type=MESH
    )

    @pl.when(seg < half_seg)
    def _():
        len_copy.start()
        for copy in mem_copies:
            copy.start()
        mid[...] = states

    @pl.when(seg >= half_seg)
    def _():
        queries = layer_norm(states, gains[0]).astype(BF)
        len_copy.wait_recv()
        col = lax.broadcasted_iota(jnp.int32, (tok, tok), 1)
        row = lax.broadcasted_iota(jnp.int32, (tok, tok), 0)
        klen_v = klen[...]
        allowed = jnp.zeros((tok, tok), jnp.bool_)
        for q in range(tok // LEN):
            inside = (col >= q * LEN) & (col - q * LEN < klen_v[q : q + 1, 0:1])
            inside = inside & (col < (q + 1) * LEN) & (row >= q * LEN) & (row < (q + 1) * LEN)
            allowed = allowed | inside
        for p in range(mem_parts):
            mem_copies[p].wait_recv()
            span_heads = range(p * heads // mem_parts, (p + 1) * heads // mem_parts)
            parts = [slice(h * HEAD_DIM, (h + 1) * HEAD_DIM) for h in span_heads]
            scores = jnp.concatenate(
                [
                    jnp.where(
                        allowed,
                        lax.dot_general(
                            queries[:, part], kmem[:, part], (((1,), (1,)), ((), ())),
                            preferred_element_type=F32,
                        )
                        * (1.0 / math.sqrt(HEAD_DIM)),
                        -1e30,
                    )
                    for part in parts
                ],
                axis=0,
            )
            top = jnp.max(scores, axis=-1, keepdims=True)
            raised = jnp.exp(scores - top)
            weights = (raised / jnp.sum(raised, axis=-1, keepdims=True)).astype(BF)
            for i, part in enumerate(parts):
                mid[:, part] = states[:, part] + jnp.dot(
                    weights[i * tok : (i + 1) * tok], kmem[:, part], preferred_element_type=F32
                )

    normed = layer_norm(mid[...], gains[1]).astype(BF)

    early[2].wait()
    expert_lane = lax.broadcasted_iota(jnp.int32, (tok, experts), 1)
    pos = lax.broadcasted_iota(jnp.int32, (tok, 1), 0)
    valid = jnp.zeros((tok, 1), F32)
    for q in range(tok // LEN):
        ok = (pos >= q * LEN) & (pos < (q + 1) * LEN) & (pos - q * LEN < lengths[0:1, q : q + 1])
        valid = valid + ok.astype(F32)
    square = lax.broadcasted_iota(jnp.int32, (tok, tok), 0) == lax.broadcasted_iota(
        jnp.int32, (tok, tok), 1
    )

    def column(row):
        spread = jnp.where(square, jnp.broadcast_to(row, (tok, tok)), 0)
        return jnp.sum(spread.astype(F32), axis=-1, keepdims=True)

    expert_lane = expert_lane.astype(F32)
    first_hot = (column(routes[0, 0:1, :]) == expert_lane).astype(F32)
    second_hot = (column(routes[0, 1:2, :]) == expert_lane).astype(F32)
    chosen = (first_hot + second_hot) * valid
    before = (
        lax.broadcasted_iota(jnp.int32, (tok, tok), 1)
        < lax.broadcasted_iota(jnp.int32, (tok, tok), 0)
    ).astype(BF)
    rank = jnp.dot(before, chosen.astype(BF), preferred_element_type=F32)
    n_main = experts * main
    n_slots = experts * cap
    lanes = -(-n_slots // 128) * 128
    lane = lax.broadcasted_iota(jnp.int32, (1, lanes), 1)
    slot_of = jnp.full((1, lanes), -1, jnp.int32)
    expert_of = jnp.full((1, lanes), -1, jnp.int32)
    for k in range(experts):
        ek = xor(e, k, experts)
        in_main = (lane >= k * main) & (lane < (k + 1) * main)
        low = n_main + k * rest
        in_rest = (lane >= low) & (lane < low + rest)
        slot_of = jnp.where(in_main, lane - k * main, slot_of)
        slot_of = jnp.where(in_rest, lane - low + main, slot_of)
        expert_of = jnp.where(in_main | in_rest, ek, expert_of)
    placing = jnp.zeros((tok, lanes), F32)
    for k in range(experts):
        here = (expert_of == k) & (rank[:, k : k + 1] == slot_of.astype(F32))
        placing = placing + jnp.where(here, chosen[:, k : k + 1], 0.0)
    place_rows = jnp.transpose(placing)[0:n_slots].astype(BF)
    slots = jnp.dot(place_rows, normed, preferred_element_type=F32)

    def place(dc, dx, k):
        turn = 0 if k in turns[0] else 1
        return turn, turn * gc + gc - 1 - dc, dx * span + turns[turn].index(k)

    def rows_a(dc, dx, k):
        _, part, b = place(dc, dx, k)
        return pl.ds(part * chunk + b * main, main)

    def index_b(dc, dx, k):
        return (dc * gx + dx) * experts + k

    x[rows_a(0, 0, 0), :] = slots[0:main].astype(BF)
    x_b[0] = slots[n_main : n_main + rest].astype(BF)
    for k in hop_order:
        out_a[k] = slots[k * main : (k + 1) * main].astype(BF)
        out_b[k] = slots[n_main + k * rest : n_main + (k + 1) * rest].astype(BF)

    waits = []

    def send(src, dst, s_sem, r_sem, target):
        copy = pltpu.make_async_remote_copy(
            src, dst, s_sem, r_sem, device_id=target, device_id_type=MESH
        )
        copy.start()
        waits.append(copy)

    def landed(ref, sem):
        pltpu.make_async_copy(ref, ref, sem).wait()

    half_width = width // 2

    def piece(slot, p):
        if p < 2:
            return x.at[rows_a(*slot), p * half_width : (p + 1) * half_width]
        return x_b.at[index_b(*slot)]

    def arrived(slot, p):
        landed(piece(slot, p), ra.at[3 * index_b(*slot) + p])

    def forward(slot_from, slot_to, p, sems, base, target):
        send(
            piece(slot_from, p), piece(slot_to, p), sems.at[3 * base + p],
            ra.at[3 * index_b(*slot_to) + p], target,
        )

    for k in hop_order:
        target = dev(xor(e, k, experts), xi, ci)
        for p in range(3):
            src = out_a.at[k, :, p * half_width : (p + 1) * half_width] if p < 2 else out_b.at[k]
            send(
                src, piece((0, 0, k), p), sz.at[3 * k + p], ra.at[3 * index_b(0, 0, k) + p], target
            )

    core_dev = dev(e, xi, lax.rem(ci + 1, gc))

    def from_column(k):
        for p in range(3):
            if k:
                arrived((0, 0, k), p)
            for d in range(1, gx):
                forward(
                    (0, 0, k), (0, d, k), p, sx, (d - 1) * experts + k,
                    dev(e, lax.rem(xi + d, gx), ci),
                )
            forward((0, 0, k), (1, 0, k), p, sc, k, core_dev)

    def from_chips(k):
        for p in range(3):
            for d in range(1, gx):
                arrived((0, d, k), p)
                forward((0, d, k), (1, d, k), p, sc, d * experts + k, core_dev)

    order = [0] + hop_order
    for i, k in enumerate(order):
        from_column(k)
        if i:
            from_chips(order[i - 1])
    from_chips(order[-1])
    for k in order:
        for d in range(gx):
            for p in range(3):
                arrived((1, d, k), p)

    blocks = gx * experts
    for dc in range(gc):
        for turn in range(len(turns)):
            for dx in range(gx):
                for k in turns[turn]:
                    _, part, b = place(dc, dx, k)
                    stage[b * rest : (b + 1) * rest, :] = x_b[index_b(dc, dx, k)].astype(F32)
            x[part * chunk + chunk_main : (part + 1) * chunk, :] = stage[...].astype(BF)

    units = win.shape[1]
    tile = min(256, units)
    loads[0].wait()

    @pl.loop(0, units // tile)
    def _(i):
        cols = pl.ds(pl.multiple_of(i * tile, tile), tile)
        act[:, cols] = jnp.maximum(
            jnp.dot(x[...], win[:, cols], preferred_element_type=F32), 0.0
        ).astype(BF)

    loads[1].wait()
    tile2 = 256

    def chip_sum(dx, k):
        turn, _, b = place(0, dx, k)
        top = turn * chunk + b * main
        sum_a = y0[top : top + main, :] + rc_a[turn, b * main : (b + 1) * main, :].astype(F32)
        low = turn * chunk + chunk_main + b * rest
        sum_b = y0[low : low + rest, :] + rc_b[turn, b].astype(F32)
        return sum_a, sum_b

    def second(turn):
        @pl.loop(0, width // tile2)
        def _(i):
            cols = pl.ds(pl.multiple_of(i * tile2, tile2), tile2)
            rows = act[turn * gc * chunk : (turn * gc + 1) * chunk, :]
            part = jnp.dot(rows, wout[:, cols], preferred_element_type=F32)
            core_a[turn, :, cols] = part[0:chunk_main].astype(BF)
            for b in range(gx * span):
                low = chunk_main + b * rest
                core_b[turn, b, :, cols] = part[low : low + rest].astype(BF)

        send(core_a.at[turn], rc_a.at[turn], rc_s.at[2 * turn], rc_r.at[2 * turn], core_dev)
        send(core_b.at[turn], rc_b.at[turn], rc_s.at[2 * turn + 1], rc_r.at[2 * turn + 1], core_dev)

        @pl.loop(0, width // tile2)
        def _(i):
            cols = pl.ds(pl.multiple_of(i * tile2, tile2), tile2)
            rows = act[(turn * gc + 1) * chunk : (turn + 1) * gc * chunk, :]
            y0[turn * chunk : (turn + 1) * chunk, cols] = jnp.dot(
                rows, wout[:, cols], preferred_element_type=F32
            )

        landed(rc_a.at[turn], rc_r.at[2 * turn])
        landed(rc_b.at[turn], rc_r.at[2 * turn + 1])
        for k in turns[turn]:
            for d in range(1, gx):
                o = (d - 1) * experts + k
                sum_a, sum_b = chip_sum(d, k)
                xs_a[o] = sum_a.astype(BF)
                xs_b[o] = sum_b.astype(BF)
                target = dev(e, lax.rem(xi + gx - d, gx), ci)
                send(xs_a.at[o], rx_a.at[o], rx_s.at[2 * o], rx_r.at[2 * o], target)
                send(xs_b.at[o], rx_b.at[o], rx_s.at[2 * o + 1], rx_r.at[2 * o + 1], target)

    second(0)
    for k in back_order:
        sum_a, sum_b = chip_sum(0, k)
        for d in range(1, gx):
            o = (d - 1) * experts + k
            landed(rx_a.at[o], rx_r.at[2 * o])
            landed(rx_b.at[o], rx_r.at[2 * o + 1])
            sum_a = sum_a + rx_a[o].astype(F32)
            sum_b = sum_b + rx_b[o].astype(F32)
        if k:
            zs_a[k] = sum_a.astype(BF)
            zs_b[k] = sum_b.astype(BF)
            target = dev(xor(e, k, experts), xi, ci)
            send(zs_a.at[k], z_a.at[k], rz_s.at[2 * k], rz_r.at[2 * k], target)
            send(zs_b.at[k], z_b.at[k], rz_s.at[2 * k + 1], rz_r.at[2 * k + 1], target)
        else:
            z_all[0:main, :] = sum_a.astype(BF)
            z_stage[0:rest, :] = sum_b

    early[3].wait()
    probs = lax.dot_general(
        normed, router[0], (((1,), (1,)), ((), ())), preferred_element_type=F32
    )
    probs = jnp.exp(probs - jnp.max(probs, axis=-1, keepdims=True))
    probs = probs / jnp.sum(probs, axis=-1, keepdims=True)
    prob_first = jnp.sum(probs * first_hot, axis=-1, keepdims=True)
    prob_second = jnp.sum(probs * second_hot, axis=-1, keepdims=True)
    gate = (prob_first * first_hot + prob_second * second_hot) / (prob_first + prob_second)
    combine = jnp.zeros((tok, lanes), F32)
    for k in range(experts):
        combine = combine + jnp.where(expert_of == k, gate[:, k : k + 1], 0.0)
    combine = (combine * placing)[:, 0:n_slots]
    high = combine.astype(BF)
    low = (combine - high.astype(F32)).astype(BF)

    early[4].wait()
    learner_in = student[0]
    shifted = learner_in - jnp.max(learner_in, axis=-1, keepdims=True)
    learner = shifted - jnp.log(jnp.sum(jnp.exp(shifted), axis=-1, keepdims=True))
    target_col = column(targets[0:1, :])
    vocab = student.shape[2]
    picked = lax.broadcasted_iota(jnp.int32, (tok, vocab), 1).astype(F32) == target_col
    hit = jnp.sum(jnp.where(picked, learner, 0.0), axis=-1, keepdims=True)
    loads[2].wait()

    for k in hop_order:
        landed(z_a.at[k], rz_r.at[2 * k])
        landed(z_b.at[k], rz_r.at[2 * k + 1])
        z_all[k * main : (k + 1) * main, :] = z_a[k]
        z_stage[k * rest : (k + 1) * rest, :] = z_b[k].astype(F32)
    z_all[n_main:, :] = z_stage[...].astype(BF)
    back = z_all[...]
    moe = jnp.dot(high, back, preferred_element_type=F32) + jnp.dot(
        low, back, preferred_element_type=F32
    )
    out = (mid[...] + moe).astype(BF)
    out_stage[...] = out
    out_copy = pltpu.make_async_copy(out_stage, layer_out.at[0], wsem.at[8])
    out_copy.start()

    final = layer_norm(out.astype(F32), gains[2]).astype(BF)
    logits = jnp.dot(final, short[...], preferred_element_type=F32)
    logits = logits - jnp.max(logits, axis=-1, keepdims=True)
    teacher = logits - jnp.log(jnp.sum(jnp.exp(logits), axis=-1, keepdims=True))
    token_loss = jnp.sum(jnp.exp(teacher) * (teacher - learner), axis=-1, keepdims=True) - hit
    counted = jnp.where(is_decoder, valid, 0.0)
    loss_sum = jnp.sum(token_loss * counted, axis=0, keepdims=True)
    loss_count = jnp.sum(counted, axis=0, keepdims=True)
    spot = lax.broadcasted_iota(jnp.int32, lsend.shape, 1)
    pair = jnp.where(spot == 0, loss_sum, jnp.where(spot == 1, loss_count, 0.0))
    lsend[...] = pair

    @pl.when(is_decoder)
    def _():
        mine = (seg - half_seg) * n_exp
        lrecv[mine + me] = pair
        for ds in range(n_seg):
            for d in range(n_exp):
                if ds or d:
                    pltpu.make_async_remote_copy(
                        lsend, lrecv.at[mine + me], l_s.at[ds * n_exp + d], l_r.at[mine + d],
                        device_id=peer(ds, d), device_id_type=MESH,
                    ).start()

    for q in range(n_seg - half_seg):
        for d in range(n_exp):
            source = q * n_exp + lax.rem(me + n_exp - d, n_exp)
            if d:
                landed(lrecv.at[source], l_r.at[q * n_exp + d])
            else:
                @pl.when(seg != q + half_seg)
                def _():
                    landed(lrecv.at[source], l_r.at[q * n_exp])

    total = lrecv[0]
    for i in range(1, (n_seg - half_seg) * n_exp):
        total = total + lrecv[i]
    loss_out[...] = total[0:1, 0:1] / total[0:1, 1:2]

    @pl.when(is_decoder)
    def _():
        for i in range(1, n_seg * n_exp):
            pltpu.make_async_copy(lsend, lsend, l_s.at[i]).wait()

    out_copy.wait()
    for copy in waits:
        copy.wait_send()

    @pl.when(seg < half_seg)
    def _():
        len_copy.wait_send()
        for copy in mem_copies:
            copy.wait_send()


def local(
    hidden, memory, lengths, memory_lengths, routes, norm_gain, router,
    w_in, w_out, shortlist, student, targets,
):
    n_seg = lax.axis_size("segment")
    n_exp = lax.axis_size("expert")
    experts = router.shape[2]
    group = n_exp // experts
    gc = 2
    gx = group // gc
    tok, width = hidden.shape[1], hidden.shape[2]
    units = w_in.shape[2]
    vocab = shortlist.shape[2]
    cap = 5 * tok // 8
    main = cap // 16 * 16
    rest = cap - main
    blocks = gx * experts
    half_rows = blocks * cap
    span = experts
    vm = pl.BlockSpec(memory_space=pltpu.VMEM)
    hbm = pl.BlockSpec(memory_space=pl.ANY)
    v = pltpu.VMEM
    dma = pltpu.SemaphoreType.DMA
    nx = max(gx - 1, 1) * experts
    scratch = [
        v((1, tok, width), BF), v((1, 2, tok), jnp.int32), v((3, 1, width), F32),
        v((1, experts, width), BF), v((1, tok, vocab), F32), v((tok, width), BF),
        v((width, units), BF), v((units, width), BF), v((width, vocab), BF),
        v((tok, width), BF), v((8, 128), jnp.int32), v((8, 128), jnp.int32), v((tok, width), F32),
        v((experts, main, width), BF), v((experts, rest, width), BF),
        v((gc * half_rows, width), BF), v((gc * blocks, rest, width), BF),
        v((gx * span * rest, width), F32), v((gc * half_rows, units), BF), v((half_rows, width), F32),
        v((1, gx * span * main, width), BF), v((1, gx * span, rest, width), BF),
        v((1, gx * span * main, width), BF), v((1, gx * span, rest, width), BF),
        v((nx, main, width), BF), v((nx, rest, width), BF),
        v((nx, main, width), BF), v((nx, rest, width), BF),
        v((experts, main, width), BF), v((experts, rest, width), BF),
        v((experts, main, width), BF), v((experts, rest, width), BF),
        v((experts * cap, width), BF), v((experts * rest, width), F32),
        v((1, 128), F32), v(((n_seg - n_seg // 2) * n_exp, 1, 128), F32),
        dma((9,)), dma((10,)), dma((3 * gc * blocks,)),
        dma((3 * experts,)), dma((3 * nx,)), dma((3 * blocks,)),
        dma((4,)), dma((4,)), dma((2 * nx,)), dma((2 * nx,)),
        dma((2 * experts,)), dma((2 * experts,)),
        dma((n_seg * n_exp,)), dma(((n_seg - n_seg // 2) * n_exp,)),
    ]
    layer_out, loss = pl.pallas_call(
        functools.partial(kernel, n_seg, n_exp, experts, gx, gc),
        out_shape=(
            jax.ShapeDtypeStruct((1, tok, width), BF),
            jax.ShapeDtypeStruct((1, 1), F32),
        ),
        in_specs=[hbm, hbm, vm, vm, hbm, hbm, hbm, hbm, hbm, hbm, hbm, vm],
        out_specs=(hbm, vm),
        scratch_shapes=scratch,
        compiler_params=pltpu.CompilerParams(
            collective_id=0, has_side_effects=True, vmem_limit_bytes=60 * 1024 * 1024
        ),
    )(
        hidden, memory, lengths, memory_lengths, jnp.swapaxes(routes, 1, 2),
        jnp.swapaxes(norm_gain, 0, 1), jnp.swapaxes(router, 1, 2),
        w_in, w_out, shortlist, student, targets,
    )
    return layer_out, loss[0, 0]


def solution(mesh):
    placed = (
        P("segment", "expert", None),
        P("segment", "expert", None),
        P("segment", "expert"),
        P("segment", "expert"),
        P("segment", "expert", None),
        P("segment", None, None),
        P("segment", None, None),
        P("segment", None, "expert"),
        P("segment", "expert", None),
        P("segment", None, None),
        P("segment", "expert", None),
        P("segment", "expert"),
    )
    return jax.shard_map(
        local,
        mesh=mesh,
        in_specs=placed,
        out_specs=(P("segment", "expert", None), P()),
        check_vma=False,
    )
```
